256 devices in a mesh: dp: 16 (over x, y), expert: 16 (over z, core).
Axes of the slice: x: 4, y: 4, z: 8, core: 2. Of those that a mesh axis runs over, the one named last changes fastest.
Arguments:
- tokens: bfloat16 [32768, 2048], P(('dp', 'expert')), may hold values from -24 to 24
- routes: int32 [32768, 2], P(('dp', 'expert')), may hold values from 0 to 7, all different within a row; in each aligned block of 128 rows (0 to 127, 128 to 255, ...) at most 36 rows name the same one
- gates: int32 [32768, 2], P(('dp', 'expert')), may hold values from 1 to 1023
- cotangent: bfloat16 [32768, 2048], P(('dp', 'expert')), may hold values from -6 to 6
- w_gate: bfloat16 [2048, 8192], P(None, 'expert'), may hold values from -0.125 to 0.125
- w_up: bfloat16 [2048, 8192], P(None, 'expert'), may hold values from -0.125 to 0.125
- w_down: bfloat16 [8192, 2048], P('expert'), may hold values from -0.1875 to 0.1875
Outputs:
- mixed: bfloat16 [32768, 2048], P(('dp', 'expert'))
- input_grad: bfloat16 [32768, 2048], P(('dp', 'expert'))
- grad_gate: float32 [2048, 8192], P('dp', 'expert')
- grad_up: float32 [2048, 8192], P('dp', 'expert')
- grad_down: float32 [8192, 2048], P('expert', 'dp')
The draws below stay inside these ranges and needn't reach their ends.
Inputs may be any that keep to these rules, and one draw needn't show every extreme that they name: `routes`: the two experts of a token differ. In the rows of one device no expert is named by more than 36 pairs, a bound that some block reaches.
All inputs are finite; a program needn't handle non-finite values.
Results may differ from the reference program's by a relative error of at most 0.0064.
Values may be sent and summed in bfloat16 or wider, within the bound.
A program may use at most 128 MiB of HBM per device.

```python
import math
import jax
import jax.numpy as jnp
import numpy as np
from jax import lax

D = 2048
FF = 1024
EXPERTS = 8
TOK_DEV = 128
CAP = 36
H = 512
TOKENS = 32768
N_EXPERT = 16


def with_ends(array, key, least, high):
    longest = array.shape.index(max(array.shape))
    spots = []
    for shift in (0, 1):
        where = [jax.random.randint(jax.random.fold_in(key, axis), (), 0, length) for axis, length in enumerate(array.shape)]
        where[longest] = (where[longest] + shift) % array.shape[longest]
        spots.append(tuple(where))
    return array.at[spots[0]].set(least).at[spots[1]].set(high)


def spiked(array, stream_key, source, target, parts, factor):
    owner, partner = [(jnp.arange(array.shape[axis_at]) // (array.shape[axis_at] // parts)).reshape([-1 if axis == axis_at else 1 for axis in range(array.ndim)]) for axis_at in (source, target)]
    chosen = jax.random.permutation(stream_key, parts)[partner]
    strong = (owner == chosen) | (owner == (partner + parts // 2) % parts)
    return jnp.where(strong, factor * array, array)


def block_scale(key, extent, cuts, low, largest):
    gain = 1.0
    for dim, parts in cuts:
        steps = jax.random.uniform(jax.random.fold_in(jax.random.fold_in(key, 6), dim), (parts,), jnp.float32, low / len(cuts), largest / len(cuts))
        gain = gain * jnp.repeat(jnp.exp(steps), extent[dim] // parts).reshape((-1,) + (1,) * (len(extent) - 1 - dim))
    return gain


def routed_block(key, own, number, rows, amount, top, reach, skew):
    order = jax.random.permutation(key, amount)
    crowded, ordinary = load_shares(amount, rows * top, reach, skew, True), load_shares(amount, rows * top, reach, skew, False)
    places = jnp.arange(amount)

    def named(lengths, rotation):
        used = int((lengths > 0).sum())
        fixed = max(1, used // 4)
        moved = fixed + (places - fixed + rotation * (used - fixed)) % max(1, amount - fixed)
        return jnp.zeros((amount,), jnp.int32).at[order[jnp.where(places < fixed, places, moved)]].set(jnp.asarray(lengths, jnp.int32))

    lengths = jnp.where(number % 4 == 0, named(crowded, number // 4), named(ordinary, number - number // 4 - 1))
    mixed = jax.random.permutation(jax.random.fold_in(own, 3), amount)
    source_of, sink = mixed[0:amount // 2 * 2:2], mixed[1:amount // 2 * 2:2]
    slack = jnp.minimum(lengths[source_of] - 1, reach - lengths[sink]) // 2
    slack = jnp.where((source_of == order[0]) | (sink == order[0]) | (lengths[sink] == 0), 0, jnp.maximum(slack, 0))
    moved = jax.random.randint(jax.random.fold_in(own, 4), (amount // 2,), 0, 1 << 20) % (slack + 1)
    lengths = lengths.at[source_of].add(-moved).at[sink].add(moved)
    members = jnp.searchsorted(jnp.cumsum(lengths), jnp.arange(rows * top), side="right").astype(jnp.int32)
    table = members.reshape(top, rows).T
    table = table[jax.random.permutation(jax.random.fold_in(own, 1), rows)]
    rotation = jax.random.randint(jax.random.fold_in(own, 2), (rows, 1), 0, top)
    return jnp.take_along_axis(table, (jnp.arange(top)[None, :] + rotation) % top, axis=1)


def load_shares(amount, total, most, skew, full):
    loads = [(1 << 20) // math.isqrt(grade ** skew) + 1 for grade in range(1, amount + 1)]
    largest = most if full else min(most, max(-(-total // amount), total * loads[0] // sum(loads)))
    least = 1 if total - largest >= amount - 1 else 0
    holding, spare = [largest] + [least] * (amount - 1), total - largest - least * (amount - 1)
    while spare > 0:
        movable = [i for i in range(1, amount) if holding[i] < largest] or [i for i in range(1, amount) if holding[i] < most]
        pool, left = sum([loads[i] for i in movable]), spare
        for i in movable:
            more = min(most - holding[i], max(1, left * loads[i] // pool), spare)
            holding[i] = holding[i] + more
            spare = spare - more
    return np.array(holding)


def normal_values(rng, dims, spread, reach, shards=(), kind=jnp.bfloat16):
    values = jax.random.normal(rng, dims, jnp.float32) * spread
    if len(shards) > 0:
        values = block_scale(rng, dims, shards, -0.22, 0.18) * values
    return jnp.clip(values, min=-reach, max=reach).astype(kind)


def gaussian_with(own_key, dims, scale, reach, shards, heavy, held_as=jnp.bfloat16):
    values = scale * jax.random.normal(own_key, dims, jnp.float32)
    if shards:
        values = values * block_scale(own_key, dims, shards, -0.22, 0.18)
    return jnp.clip(spiked(values, jax.random.fold_in(own_key, 3), *heavy), -reach, reach).astype(held_as)


def setup_inputs(seed: int = 0) -> dict:
    arg_keys = jax.random.split(jax.random.key(seed), 8)
    tokens = gaussian_with(arg_keys[0], (TOKENS, D), 1.0, 24.0, ((0, 256),), (0, 1, 256, 6.0))
    routes_keys = jax.random.split(jax.random.fold_in(arg_keys[1], 1), TOKENS // TOK_DEV)
    routes_turns = jax.random.permutation(jax.random.fold_in(arg_keys[1], 3), TOKENS // TOK_DEV)
    routes = jax.vmap(lambda own, number: routed_block(jax.random.fold_in(arg_keys[1], 2), own, number, TOK_DEV, EXPERTS, 2, CAP, 2))(routes_keys, routes_turns).reshape((TOKENS, 2))
    gates = with_ends(jax.random.randint(arg_keys[2], (TOKENS, 2), 1, 1024), jax.random.fold_in(arg_keys[2], 1), 1, 1023).astype(jnp.int32)
    cotangent = normal_values(arg_keys[3], (TOKENS, D), 1.0, 6.0, ((0, 256),))
    w_gate = normal_values(arg_keys[4], (D, EXPERTS * FF), D ** -0.5, 0.125, ((1, 16),))
    w_up = normal_values(arg_keys[5], (D, EXPERTS * FF), D ** -0.5, 0.125, ((1, 16),))
    w_down = normal_values(arg_keys[6], (EXPERTS * FF, D), FF ** -0.5, 0.1875, ((0, 16),))
    return {"tokens": tokens, "routes": routes, "gates": gates, "cotangent": cotangent, "w_gate": w_gate, "w_up": w_up, "w_down": w_down}


def local_table(pairs):
    count = pairs.shape[0]
    onehot = (pairs[:, None] == jnp.arange(EXPERTS, dtype=jnp.int32)[None, :]).astype(jnp.int32)
    before = jnp.cumsum(onehot, axis=0) - onehot
    position = jnp.sum(before * onehot, axis=1).astype(jnp.int32)
    table = jnp.full((EXPERTS * CAP,), count, jnp.int32)
    return table.at[pairs * CAP + position].set(jnp.arange(count, dtype=jnp.int32))


def reference(tokens, routes, gates, cotangent, w_gate, w_up, w_down):
    blocks = TOKENS // TOK_DEV
    per = 2 * TOK_DEV
    tiles = N_EXPERT // EXPERTS
    tables = jax.vmap(local_table)(routes.reshape(blocks, per).astype(jnp.int32))
    offsets = (jnp.arange(blocks, dtype=jnp.int32) * per)[:, None]
    global_ids = jnp.where(tables < per, tables + offsets, 2 * TOKENS).astype(jnp.int32).reshape(blocks, EXPERTS, CAP)
    factor = jnp.concatenate([gates.reshape(-1).astype(jnp.float32) / 1024.0, jnp.zeros((1,), jnp.float32)])
    padded_x = jnp.concatenate([tokens, jnp.zeros((1, D), jnp.bfloat16)])
    padded_dy = jnp.concatenate([cotangent, jnp.zeros((1, D), jnp.bfloat16)])
    mixed_acc = jnp.zeros((TOKENS + 1, D), jnp.float32)
    dx_acc = jnp.zeros((TOKENS + 1, D), jnp.float32)
    gate_list, up_list, down_list = [], [], []
    for expert in range(EXPERTS):
        ids = global_ids[:, expert, :].reshape(-1)
        rows_tok = (ids // 2).astype(jnp.int32)
        xrows = padded_x[rows_tok]
        scale = factor[ids]
        dz = (scale[:, None] * padded_dy[rows_tok].astype(jnp.float32)).astype(jnp.bfloat16)
        for part in range(tiles):
            col = (expert * tiles + part) * H
            wg = w_gate[:, col:col + H]
            wu = w_up[:, col:col + H]
            wd = w_down[col:col + H, :]
            a = jnp.dot(xrows, wg, preferred_element_type=jnp.float32)
            b = jnp.dot(xrows, wu, preferred_element_type=jnp.float32)
            sig = jax.nn.sigmoid(a)
            act = a * sig
            h = (act * b).astype(jnp.bfloat16)
            z = jnp.dot(h, wd, preferred_element_type=jnp.float32).astype(jnp.bfloat16)
            mixed_acc = mixed_acc.at[rows_tok].add(scale[:, None] * z.astype(jnp.float32))
            dh = lax.dot_general(dz, wd, (((1,), (1,)), ((), ())), preferred_element_type=jnp.float32)
            dsilu = sig * (1.0 + a * (1.0 - sig))
            d_gate = (dh * b * dsilu).astype(jnp.bfloat16)
            d_up = (dh * act).astype(jnp.bfloat16)
            dx = lax.dot_general(d_gate, wg, (((1,), (1,)), ((), ())), preferred_element_type=jnp.float32)
            dx = dx + lax.dot_general(d_up, wu, (((1,), (1,)), ((), ())), preferred_element_type=jnp.float32)
            dx_acc = dx_acc.at[rows_tok].add(dx.astype(jnp.bfloat16).astype(jnp.float32))
            gate_list.append(lax.dot_general(xrows, d_gate, (((0,), (0,)), ((), ())), preferred_element_type=jnp.float32))
            up_list.append(lax.dot_general(xrows, d_up, (((0,), (0,)), ((), ())), preferred_element_type=jnp.float32))
            down_list.append(lax.dot_general(h, dz, (((0,), (0,)), ((), ())), preferred_element_type=jnp.float32))
    mixed = mixed_acc[:TOKENS].astype(jnp.bfloat16)
    input_grad = dx_acc[:TOKENS].astype(jnp.bfloat16)
    grad_gate = jnp.concatenate(gate_list, axis=1)
    grad_up = jnp.concatenate(up_list, axis=1)
    grad_down = jnp.concatenate(down_list, axis=0)
    return (mixed, input_grad, grad_gate, grad_up, grad_down)
```

```python
import jax
import jax.numpy as jnp
from jax import lax
from jax.experimental import pallas as pl
from jax.experimental.pallas import tpu as pltpu
from jax.sharding import PartitionSpec as P

MESH = pl.DeviceIdType.MESH
BF16 = jnp.bfloat16
F32 = jnp.float32

T = 128
D = 2048
H = 512
E = 8
MAIN = 32
REM = 4
W = 512
J = D // W
BLK = J * MAIN + J * REM
ROWS = 2 * E * (MAIN + REM)
HALF = 80
Q = 384


def dot(a, b):
    return jnp.dot(a, b, preferred_element_type=F32)


def dot_rows(a, b):
    return lax.dot_general(a, b, (((0,), (0,)), ((), ())), preferred_element_type=F32)


def dot_cols(a, b):
    return lax.dot_general(a, b, (((1,), (1,)), ((), ())), preferred_element_type=F32)


def kernel(
    routes,
    gates,
    tokens,
    cotangent,
    w_gate,
    w_up,
    w_down,
    mixed,
    input_grad,
    grad_gate,
    grad_up,
    grad_down,
    wgu,
    wd,
    gx,
    gxr,
    gf,
    gfr,
    perm,
    send,
    xr,
    zr,
    back,
    relay_a,
    relay_b,
    xrows,
    dzrows,
    act_s,
    dact_s,
    h_s,
    bg,
    own_s,
    part_out,
    part_in,
    g_s,
    a_recv,
    a_send,
    a_tot,
    b_recv,
    b_send,
    load_sem,
    local_sem,
    ssem,
    rsem,
):
    dp = lax.axis_index("dp")
    ex = lax.axis_index("expert")
    z, core = ex // 2, ex % 2
    x, y = dp // 4, dp % 4

    def zz(d):
        return (z + d + 8) % 8

    def zdev(d):
        return (dp, zz(d) * 2 + core)

    partner = (dp, z * 2 + (1 - core))

    def ring_dev(along_x, d):
        if along_x:
            return (((x + d + 4) % 4) * 4 + y, ex)
        return (x * 4 + (y + d + 4) % 4, ex)

    barrier = pltpu.get_barrier_semaphore()
    peers = [zdev(d) for d in range(1, 8)] + [partner]
    peers += [ring_dev(True, 1), ring_dev(True, -1), ring_dev(False, 1), ring_dev(False, -1)]
    for peer in peers:
        pl.semaphore_signal(barrier, inc=1, device_id=peer, device_id_type=MESH)

    loads = [
        pltpu.make_async_copy(w_gate, wgu.at[:, pl.ds(0, H)], load_sem.at[0]),
        pltpu.make_async_copy(w_up, wgu.at[:, pl.ds(H, H)], load_sem.at[1]),
        pltpu.make_async_copy(w_down, wd, load_sem.at[2]),
    ]
    for load in loads:
        load.start()

    row16 = lax.broadcasted_iota(jnp.int32, (16, T), 0)
    first = row16 == routes[0:1, :]
    second = row16 == routes[1:2, :]
    named = jnp.logical_or(first, second)
    earlier = lax.broadcasted_iota(jnp.int32, (T, T), 0) < lax.broadcasted_iota(jnp.int32, (T, T), 1)
    before = dot(
        jnp.where(named, 1.0, 0.0).astype(BF16), jnp.where(earlier, 1.0, 0.0).astype(BF16)
    ).astype(jnp.int32)
    slot = jnp.where(named, before, -1)
    gate = jnp.where(first, gates[0:1, :], 0) + jnp.where(second, gates[1:2, :], 0)
    high = ((gate >> 3) << 3).astype(F32) * (1.0 / 1024.0)
    low = (gate & 7).astype(F32) * (1.0 / 1024.0)
    rowm = lax.broadcasted_iota(jnp.int32, (MAIN, T), 0)
    rowr = lax.broadcasted_iota(jnp.int32, (J * REM, T), 0)
    for e in range(E):
        at = slot[e : e + 1, :]
        hi, lo = high[e : e + 1, :], low[e : e + 1, :]
        hit = rowm == at
        gx[pl.ds(e * MAIN, MAIN), :] = jnp.where(hit, 1.0, 0.0).astype(BF16)
        gf[pl.ds(e * MAIN, MAIN), pl.ds(0, T)] = jnp.where(hit, hi, 0.0).astype(BF16)
        gf[pl.ds(e * MAIN, MAIN), pl.ds(T, T)] = jnp.where(hit, lo, 0.0).astype(BF16)
        hitr = (MAIN + (rowr & (REM - 1))) == at
        for j in range(J):
            hitj = jnp.logical_and(hitr, (rowr >> 2) == j)
            rows = pl.ds(e * J * REM, J * REM)
            gxr[j, rows, :] = jnp.where(hitj, 1.0, 0.0).astype(BF16)
            gfr[j, rows, pl.ds(0, T)] = jnp.where(hitj, hi, 0.0).astype(BF16)
            gfr[j, rows, pl.ds(T, T)] = jnp.where(hitj, lo, 0.0).astype(BF16)
    pr = lax.broadcasted_iota(jnp.int32, (E * REM, E * J * REM), 0)
    pc = lax.broadcasted_iota(jnp.int32, (E * REM, E * J * REM), 1)
    for j in range(J):
        same = jnp.logical_and(pr >> 2 == pc >> 4, (pc & 15) == j * REM + (pr & 3))
        perm[j] = jnp.where(same, 1.0, 0.0).astype(BF16)

    def cols(j):
        return pl.ds(pl.multiple_of(j * W, W), W)

    def main_rows(j):
        return pl.ds(pl.multiple_of(j * MAIN, MAIN), MAIN)

    def pack(buf, j, rows):
        buf[:, main_rows(j), :] = rows.reshape(E, MAIN, W)

    def pack_rest(buf, rest):
        buf[:, pl.ds(J * MAIN, J * REM), :] = rest.astype(BF16).reshape(E, J * REM, W)

    def rest_of(buf):
        return buf[:, pl.ds(J * MAIN, J * REM), :].reshape(E * J * REM, W)

    def gather_x(j, rest):
        piece = tokens[:, cols(j)]
        pack(send.at[0], j, dot(gx[...], piece).astype(BF16))
        return rest + dot(gxr[j], piece)

    def gather_dz(j, rest):
        piece = cotangent[:, cols(j)]
        both = jnp.concatenate([piece, piece], axis=0)
        pack(send.at[1], j, dot(gf[...], both).astype(BF16))
        return rest + dot(gfr[j], both)

    zero_rest = jnp.zeros((E * J * REM, W), F32)

    def remote(src, dst, index, device):
        return pltpu.make_async_remote_copy(
            src_ref=src,
            dst_ref=dst,
            send_sem=ssem.at[index],
            recv_sem=rsem.at[index],
            device_id=device,
            device_id_type=MESH,
        )

    started = []

    def start(copies):
        for copy in copies:
            copy.start()
            started.append(copy)

    class Exchange:
        def __init__(self, k, recv):
            src, ra, rb = send.at[k], relay_a.at[k], relay_b.at[k]
            base = 10 * k
            far = zz(4)
            upper, lower = pl.ds(0, HALF), pl.ds(HALF, BLK - HALF)
            self.legs = [
                remote(src.at[far, upper], ra, base, zdev(2)),
                remote(src.at[far, lower], rb, base + 1, zdev(-2)),
            ]
            self.direct = [
                remote(src.at[zz(d)], recv.at[z], base + 2 + n, zdev(d))
                for n, d in enumerate((3, -3, 2, -2, 1, -1))
            ]
            self.onward = [
                remote(ra, recv.at[zz(-2), upper], base + 8, zdev(2)),
                remote(rb, recv.at[zz(2), lower], base + 9, zdev(-2)),
            ]
            self.own = pltpu.make_async_copy(src.at[z], recv.at[z], local_sem.at[k])

        def begin(self):
            start(self.legs)
            start(self.direct)
            self.own.start()

        def pass_on(self):
            for leg, copy in zip(self.legs, self.onward):
                leg.wait_recv()
                start([copy])

        def arrived(self):
            for copy in self.direct + self.onward:
                copy.wait_recv()
            self.own.wait()

    def unpack(got, rows):
        for g in range(2):

            def one(j, carry):
                rows[pl.ds(g * E * MAIN, E * MAIN), cols(j)] = got[g, :, main_rows(j), :].reshape(
                    E * MAIN, W
                )
                rest = dot(perm[j], rest_of(got.at[g])).astype(BF16)
                rows[pl.ds(2 * E * MAIN + g * E * REM, E * REM), cols(j)] = rest
                return carry

            lax.fori_loop(0, J, one, 0)

    om, orr = pl.ds(0, E * MAIN), pl.ds(E * MAIN, E * REM)

    def partials(k, product):
        def one(j, rest):
            value = product(j)
            n = E * MAIN
            pack(part_out.at[k], j, value[n : 2 * n].astype(BF16))
            own_s[om, cols(j)] = value[0:n]
            own_s[orr, cols(j)] = value[2 * n : 2 * n + E * REM]
            return rest + dot_rows(perm[j], value[2 * n + E * REM :].astype(BF16))

        pack_rest(part_out.at[k], lax.fori_loop(0, J, one, zero_rest))
        swap = remote(part_out.at[k], part_in.at[k], 42 + k, partner)
        start([swap])
        return swap

    def add_partials(k, to):
        def one(j, rest):
            got = part_in[k, :, main_rows(j), :].reshape(E * MAIN, W).astype(F32)
            pack(send.at[to], j, (own_s[om, cols(j)] + got).astype(BF16))
            more = own_s[orr, cols(j)] + dot(perm[j], rest_of(part_in.at[k]))
            return rest + dot_rows(perm[j], more.astype(BF16))

        pack_rest(send.at[to], lax.fori_loop(0, J, one, zero_rest))

    ex_x, ex_dz = Exchange(0, xr.at[0]), Exchange(1, zr.at[0])
    ex_z, ex_dx = Exchange(2, back.at[0]), Exchange(3, back.at[1])

    pack_rest(send.at[0], lax.fori_loop(0, J, gather_x, zero_rest))
    pl.semaphore_wait(barrier, len(peers))
    ex_x.begin()
    pack_rest(send.at[1], lax.fori_loop(0, J, gather_dz, zero_rest))
    ex_x.pass_on()
    ex_dz.begin()
    ex_x.arrived()
    swap_x = remote(xr.at[0], xr.at[1], 40, partner)
    start([swap_x])
    for load in loads:
        load.wait()
    swap_x.wait_recv()

    unpack(xr, xrows)

    def forward(n, carry):
        at = pl.ds(pl.multiple_of(n * 256, 256), 256)
        upat = pl.ds(pl.multiple_of(H + n * 256, 256), 256)
        a = dot(xrows[...], wgu[:, at])
        b = dot(xrows[...], wgu[:, upat])
        sig = jax.nn.sigmoid(a)
        act = a * sig
        h_s[:, at] = (act * b).astype(BF16)
        act_s[:, at] = act
        dact_s[:, at] = b * (sig * (1.0 + a * (1.0 - sig)))
        return carry

    lax.fori_loop(0, H // 256, forward, 0)
    swap = partials(0, lambda j: dot(h_s[...], wd[:, cols(j)]))
    ex_dz.pass_on()
    swap.wait_recv()
    add_partials(0, 2)
    ex_z.begin()

    ex_dz.arrived()
    swap_dz = remote(zr.at[0], zr.at[1], 41, partner)
    start([swap_dz])
    ex_z.pass_on()
    swap_dz.wait_recv()
    unpack(zr, dzrows)

    def backward(n, carry):
        at = pl.ds(pl.multiple_of(n * 256, 256), 256)
        upat = pl.ds(pl.multiple_of(H + n * 256, 256), 256)
        dh = dot_cols(dzrows[...], wd[at, :])
        bg[:, at] = (dh * dact_s[:, at]).astype(BF16)
        bg[:, upat] = (dh * act_s[:, at]).astype(BF16)
        return carry

    lax.fori_loop(0, H // 256, backward, 0)

    def grads(p, carry):
        at = pl.ds(pl.multiple_of(p * 256, 256), 256)
        both = dot_rows(xrows[:, at], bg[...]).astype(BF16)
        down = dot_rows(dzrows[:, at], h_s[...]).astype(BF16)
        px, py = p // 2, (p % 2) * 2
        for i in range(2):
            rows = slice(i * 128, (i + 1) * 128)
            g_s[0, px, py + i] = both[rows, 0:Q]
            g_s[1, px, py + i] = both[rows, Q : 2 * Q]
            g_s[2, px, py + i, :, pl.ds(0, 256)] = both[rows, 2 * Q : 1024]
            g_s[2, px, py + i, :, pl.ds(256, 128)] = down[rows, 0:128]
            g_s[3, px, py + i] = down[rows, 128:512]
        return carry

    lax.fori_loop(0, 8, grads, 0)

    class Ring:
        def __init__(self, k, along_x, part, recv, out):
            self.recv, self.part, self.out = recv, part, out
            self.me = x if along_x else y
            base = 44 + 6 * k
            right, left = ring_dev(along_x, 1), ring_dev(along_x, -1)
            self.legs = [
                remote(part(0, self.at(2)), recv.at[0], base, right),
                remote(part(1, self.at(2)), recv.at[1], base + 1, left),
            ]
            self.direct = [
                remote(part(1, self.at(1)), recv.at[2], base + 2, right),
                remote(part(0, self.at(-1)), recv.at[3], base + 3, left),
            ]
            self.sums = [
                remote(out.at[0], recv.at[4], base + 4, right),
                remote(out.at[1], recv.at[5], base + 5, left),
            ]

        def at(self, d):
            return (self.me + d + 4) % 4

        def begin(self):
            start(self.legs)
            start(self.direct)

        def relay(self):
            for side, d in ((0, 1), (1, -1)):
                self.legs[side].wait_recv()
                mine = self.part(side, self.at(d))[...].astype(F32)
                self.out[side] = (mine + self.recv[side].astype(F32)).astype(BF16)
                start([self.sums[side]])

        def total(self, side):
            mine = self.part(side, self.me)[...].astype(F32)
            other = self.recv[3 - side].astype(F32)
            return mine + other + self.recv[4 + side].astype(F32)

        def arrived(self):
            for copy in self.direct + self.sums:
                copy.wait_recv()

    ring_a = [
        Ring(0, True, lambda s, p: g_s.at[s, p], a_recv.at[0], a_send.at[0]),
        Ring(1, False, lambda s, p: g_s.at[2 + s, :, p], a_recv.at[1], a_send.at[1]),
    ]
    ring_b = [
        Ring(2, False, lambda s, p: a_tot.at[0, s, p], b_recv.at[0], b_send.at[0]),
        Ring(3, True, lambda s, p: a_tot.at[1, s, p], b_recv.at[1], b_send.at[1]),
    ]
    for ring in ring_a:
        ring.begin()

    swap = partials(1, lambda j: dot_cols(bg[...], wgu[cols(j), :]))
    for ring in ring_a:
        ring.relay()
    swap.wait_recv()
    add_partials(1, 3)
    ex_dx.begin()

    def combine(k, out, left, rest_left):
        def one(j, carry):
            rows = back[k, :, main_rows(j), :].reshape(E * MAIN, W)
            value = dot_rows(left[...], rows) + dot_rows(rest_left[j], rest_of(back.at[k]))
            if left.shape[1] == 2 * T:
                value = value[0:T] + value[T:]
            out[:, cols(j)] = value.astype(BF16)
            return carry

        lax.fori_loop(0, J, one, 0)

    ex_z.arrived()
    combine(0, mixed, gf, gfr)
    ex_dx.pass_on()

    for k, ring in enumerate(ring_a):
        ring.arrived()
        for side in range(2):
            a_tot[k, side] = ring.total(side).astype(BF16)
        ring_b[k].begin()
    for ring in ring_b:
        ring.relay()
    quarters = []
    for ring in ring_b:
        ring.arrived()
        quarters += [ring.total(0), ring.total(1)]
    q0, q1, q2, q3 = quarters
    grad_gate[:, pl.ds(0, Q)] = q0
    grad_gate[:, pl.ds(Q, H - Q)] = q1[:, 0:128]
    grad_up[:, pl.ds(0, 256)] = q1[:, 128:Q]
    grad_up[:, pl.ds(256, 256)] = q2[:, 0:256]
    grad_down[pl.ds(0, 128), :] = q2[:, 256:Q].T
    grad_down[pl.ds(128, Q), :] = q3.T

    ex_dx.arrived()
    combine(1, input_grad, gx, gxr)
    for copy in started:
        copy.wait_send()


def per_device(tokens, routes, gates, cotangent, w_gate, w_up, w_down):
    vmem = pl.BlockSpec(memory_space=pltpu.VMEM)
    hbm = pl.BlockSpec(memory_space=pl.ANY)
    half = (4, 128, Q)
    return pl.pallas_call(
        kernel,
        out_shape=(
            jax.ShapeDtypeStruct((T, D), BF16),
            jax.ShapeDtypeStruct((T, D), BF16),
            jax.ShapeDtypeStruct((128, H), F32),
            jax.ShapeDtypeStruct((128, H), F32),
            jax.ShapeDtypeStruct((H, 128), F32),
        ),
        in_specs=[vmem] * 4 + [hbm] * 3,
        out_specs=(vmem,) * 5,
        scratch_shapes=[
            pltpu.VMEM((D, 2 * H), BF16),
            pltpu.VMEM((H, D), BF16),
            pltpu.VMEM((E * MAIN, T), BF16),
            pltpu.VMEM((J, E * J * REM, T), BF16),
            pltpu.VMEM((E * MAIN, 2 * T), BF16),
            pltpu.VMEM((J, E * J * REM, 2 * T), BF16),
            pltpu.VMEM((J, E * REM, E * J * REM), BF16),
            pltpu.VMEM((4, E, BLK, W), BF16),
            pltpu.VMEM((2, E, BLK, W), BF16),
            pltpu.VMEM((2, E, BLK, W), BF16),
            pltpu.VMEM((2, E, BLK, W), BF16),
            pltpu.VMEM((4, HALF, W), BF16),
            pltpu.VMEM((4, BLK - HALF, W), BF16),
            pltpu.VMEM((ROWS, D), BF16),
            pltpu.VMEM((ROWS, D), BF16),
            pltpu.VMEM((ROWS, H), F32),
            pltpu.VMEM((ROWS, H), F32),
            pltpu.VMEM((ROWS, H), BF16),
            pltpu.VMEM((ROWS, 2 * H), BF16),
            pltpu.VMEM((E * (MAIN + REM), D), F32),
            pltpu.VMEM((2, E, BLK, W), BF16),
            pltpu.VMEM((2, E, BLK, W), BF16),
            pltpu.VMEM((4, 4, 4, 128, Q), BF16),
            pltpu.VMEM((2, 6) + half, BF16),
            pltpu.VMEM((2, 2) + half, BF16),
            pltpu.VMEM((2, 2) + half, BF16),
            pltpu.VMEM((2, 6, 128, Q), BF16),
            pltpu.VMEM((2, 2, 128, Q), BF16),
            pltpu.SemaphoreType.DMA((3,)),
            pltpu.SemaphoreType.DMA((4,)),
            pltpu.SemaphoreType.DMA((68,)),
            pltpu.SemaphoreType.DMA((68,)),
        ],
        compiler_params=pltpu.CompilerParams(
            collective_id=0, has_side_effects=True, vmem_limit_bytes=63_000_000
        ),
        name="moe",
    )(routes.T, gates.T, tokens, cotangent, w_gate, w_up, w_down)


def solution(mesh):
    in_specs = (
        P(("dp", "expert"), None),
        P(("dp", "expert"), None),
        P(("dp", "expert"), None),
        P(("dp", "expert"), None),
        P(None, "expert"),
        P(None, "expert"),
        P("expert", None),
    )
    out_specs = (
        P(("dp", "expert"), None),
        P(("dp", "expert"), None),
        P("dp", "expert"),
        P("dp", "expert"),
        P("expert", "dp"),
    )
    return jax.shard_map(
        per_device, mesh=mesh, in_specs=in_specs, out_specs=out_specs, check_vma=False
    )
```

```python
import jax
import jax.numpy as jnp
from jax import lax
from jax.experimental import pallas as pl
from jax.experimental.pallas import tpu as pltpu
from jax.sharding import PartitionSpec as P

MESH = pl.DeviceIdType.MESH
BF16 = jnp.bfloat16
F32 = jnp.float32

T = 128
D = 2048
H = 512
E = 8
MAIN = 32
REM = 4
W = 512
J = D // W
BLK = J * MAIN + J * REM
ROWS = 2 * E * (MAIN + REM)
Q = 384


def dot(a, b):
    return jnp.dot(a, b, preferred_element_type=F32)


def dot_rows(a, b):
    return lax.dot_general(a, b, (((0,), (0,)), ((), ())), preferred_element_type=F32)


def dot_cols(a, b):
    return lax.dot_general(a, b, (((1,), (1,)), ((), ())), preferred_element_type=F32)


def kernel(
    routes,
    gates,
    tokens_in,
    cotangent_in,
    w_gate,
    w_up,
    w_down,
    mixed_out,
    dx_back,
    left_out,
    left_rest_out,
    grad_gate_out,
    grad_up_out,
    grad_down_out,
    tokens,
    cotangent,
    mixed,
    grad_gate,
    grad_up,
    grad_down,
    left,
    left_rest,
    wgu,
    wd,
    gx,
    gxr,
    gf,
    gfr,
    perm,
    send,
    xr,
    zr,
    back,
    xrows,
    dzrows,
    act_s,
    dact_s,
    h_s,
    bg,
    own_s,
    part_out,
    part_in,
    g_s,
    a_recv,
    a_send,
    a_tot,
    b_recv,
    b_send,
    load_sem,
    store_sem,
    local_sem,
    ssem,
    rsem,
):
    dp = lax.axis_index("dp")
    ex = lax.axis_index("expert")
    z, core = ex // 2, ex % 2
    x, y = dp // 4, dp % 4

    def zz(d):
        return (z + d + 8) % 8

    def zdev(d):
        return (dp, zz(d) * 2 + core)

    partner = (dp, z * 2 + (1 - core))

    def ring_dev(along_x, d):
        if along_x:
            return (((x + d + 4) % 4) * 4 + y, ex)
        return (x * 4 + (y + d + 4) % 4, ex)

    barrier = pltpu.get_barrier_semaphore()
    peers = [zdev(d) for d in range(1, 8)] + [partner]
    peers += [ring_dev(True, 1), ring_dev(True, -1), ring_dev(False, 1), ring_dev(False, -1)]
    for peer in peers:
        pl.semaphore_signal(barrier, inc=1, device_id=peer, device_id_type=MESH)

    load_x = pltpu.make_async_copy(tokens_in, tokens, load_sem.at[3])
    load_dy = pltpu.make_async_copy(cotangent_in, cotangent, load_sem.at[4])
    loads = [
        pltpu.make_async_copy(w_gate, wgu.at[:, pl.ds(0, H)], load_sem.at[0]),
        pltpu.make_async_copy(w_up, wgu.at[:, pl.ds(H, H)], load_sem.at[1]),
        pltpu.make_async_copy(w_down, wd, load_sem.at[2]),
    ]
    for load in [load_x, load_dy] + loads:
        load.start()

    row16 = lax.broadcasted_iota(jnp.int32, (16, T), 0)
    first = row16 == routes[0:1, :]
    second = row16 == routes[1:2, :]
    named = jnp.logical_or(first, second)
    earlier = lax.broadcasted_iota(jnp.int32, (T, T), 0) < lax.broadcasted_iota(jnp.int32, (T, T), 1)
    before = dot(
        jnp.where(named, 1.0, 0.0).astype(BF16), jnp.where(earlier, 1.0, 0.0).astype(BF16)
    ).astype(jnp.int32)
    slot = jnp.where(named, before, -1)
    gate = jnp.where(first, gates[0:1, :], 0) + jnp.where(second, gates[1:2, :], 0)
    high = ((gate >> 3) << 3).astype(F32) * (1.0 / 1024.0)
    low = (gate & 7).astype(F32) * (1.0 / 1024.0)
    rowm = lax.broadcasted_iota(jnp.int32, (MAIN, T), 0)
    rowr = lax.broadcasted_iota(jnp.int32, (J * REM, T), 0)
    def hits(e, j):
        if j is None:
            return rowm == slot[e : e + 1, :]
        hit = (MAIN + (rowr & (REM - 1))) == slot[e : e + 1, :]
        return jnp.logical_and(hit, (rowr >> 2) == j)

    for e in range(E):
        gx[pl.ds(e * MAIN, MAIN), :] = jnp.where(hits(e, None), 1.0, 0.0).astype(BF16)
        for j in range(J):
            rows = pl.ds(e * J * REM, J * REM)
            gxr[j, rows, :] = jnp.where(hits(e, j), 1.0, 0.0).astype(BF16)

    def scaled_masks():
        for e in range(E):
            for n, part in enumerate((high[e : e + 1, :], low[e : e + 1, :])):
                lanes = pl.ds(n * T, T)
                gf[pl.ds(e * MAIN, MAIN), lanes] = jnp.where(hits(e, None), part, 0.0).astype(BF16)
                for j in range(J):
                    rows = pl.ds(e * J * REM, J * REM)
                    gfr[j, rows, lanes] = jnp.where(hits(e, j), part, 0.0).astype(BF16)

    def other_masks():
        pr = lax.broadcasted_iota(jnp.int32, (E * REM, E * J * REM), 0)
        pc = lax.broadcasted_iota(jnp.int32, (E * REM, E * J * REM), 1)
        for j in range(J):
            same = jnp.logical_and(pr >> 2 == pc >> 4, (pc & 15) == j * REM + (pr & 3))
            perm[j] = jnp.where(same, 1.0, 0.0).astype(BF16)
            left_rest[j] = gxr[j].astype(F32).T.astype(BF16)
        left[...] = gx[...].astype(F32).T.astype(BF16)

    def cols(j):
        return pl.ds(pl.multiple_of(j * W, W), W)

    def main_rows(j):
        return pl.ds(pl.multiple_of(j * MAIN, MAIN), MAIN)

    def pack(buf, j, rows):
        buf[:, main_rows(j), :] = rows.reshape(E, MAIN, W)

    def pack_rest(buf, rest):
        buf[:, pl.ds(J * MAIN, J * REM), :] = rest.astype(BF16).reshape(E, J * REM, W)

    def rest_of(buf):
        return buf[:, pl.ds(J * MAIN, J * REM), :].reshape(E * J * REM, W)

    def gather_x(j, rest):
        piece = tokens[:, cols(j)]
        pack(send.at[0], j, dot(gx[...], piece).astype(BF16))
        return rest + dot(gxr[j], piece)

    def gather_dz(j, rest):
        piece = cotangent[:, cols(j)]
        both = jnp.concatenate([piece, piece], axis=0)
        pack(send.at[1], j, dot(gf[...], both).astype(BF16))
        return rest + dot(gfr[j], both)

    zero_rest = jnp.zeros((E * J * REM, W), F32)

    def remote(src, dst, index, device):
        return pltpu.make_async_remote_copy(
            src_ref=src,
            dst_ref=dst,
            send_sem=ssem.at[index],
            recv_sem=rsem.at[index],
            device_id=device,
            device_id_type=MESH,
        )

    started = []

    def start(copies):
        for copy in copies:
            copy.start()
            started.append(copy)

    class Exchange:
        def __init__(self, k, recv):
            src = send.at[k]
            self.copies = [
                remote(src.at[zz(d)], recv.at[z], 7 * k + n, zdev(d))
                for n, d in enumerate((4, 3, -3, 2, -2, 1, -1))
            ]
            self.own = pltpu.make_async_copy(src.at[z], recv.at[z], local_sem.at[k])

        def begin(self):
            start(self.copies)
            self.own.start()

        def arrived(self):
            for copy in self.copies:
                copy.wait_recv()
            self.own.wait()

    def unpack(got, rows):
        for g in range(2):

            def one(j, carry):
                rows[pl.ds(g * E * MAIN, E * MAIN), cols(j)] = got[g, :, main_rows(j), :].reshape(
                    E * MAIN, W
                )
                rest = dot(perm[j], rest_of(got.at[g])).astype(BF16)
                rows[pl.ds(2 * E * MAIN + g * E * REM, E * REM), cols(j)] = rest
                return carry

            lax.fori_loop(0, J, one, 0)

    om, orr = pl.ds(0, E * MAIN), pl.ds(E * MAIN, E * REM)

    def partials(k, product):
        def one(j, rest):
            value = product(j)
            n = E * MAIN
            pack(part_out.at[k], j, value[n : 2 * n].astype(BF16))
            own_s[om, cols(j)] = value[0:n]
            own_s[orr, cols(j)] = value[2 * n : 2 * n + E * REM]
            return rest + dot_rows(perm[j], value[2 * n + E * REM :].astype(BF16))

        pack_rest(part_out.at[k], lax.fori_loop(0, J, one, zero_rest))
        swap = remote(part_out.at[k], part_in.at[k], 30 + k, partner)
        start([swap])
        return swap

    def add_partials(k, to):
        def one(j, rest):
            got = part_in[k, :, main_rows(j), :].reshape(E * MAIN, W).astype(F32)
            pack(send.at[to], j, (own_s[om, cols(j)] + got).astype(BF16))
            more = own_s[orr, cols(j)] + dot(perm[j], rest_of(part_in.at[k]))
            return rest + dot_rows(perm[j], more.astype(BF16))

        pack_rest(send.at[to], lax.fori_loop(0, J, one, zero_rest))

    ex_x, ex_dz = Exchange(0, xr.at[0]), Exchange(1, zr.at[0])
    ex_z, ex_dx = Exchange(2, back), Exchange(3, dx_back)

    load_x.wait()
    pack_rest(send.at[0], lax.fori_loop(0, J, gather_x, zero_rest))
    pl.semaphore_wait(barrier, len(peers))
    ex_x.begin()
    scaled_masks()
    load_dy.wait()
    pack_rest(send.at[1], lax.fori_loop(0, J, gather_dz, zero_rest))
    ex_dz.begin()
    other_masks()
    stores = [
        pltpu.make_async_copy(left, left_out, store_sem.at[0]),
        pltpu.make_async_copy(left_rest, left_rest_out, store_sem.at[1]),
    ]
    for store in stores:
        store.start()
    ex_x.arrived()
    swap_x = remote(xr.at[0], xr.at[1], 28, partner)
    start([swap_x])
    for load in loads:
        load.wait()
    swap_x.wait_recv()

    unpack(xr, xrows)

    def forward(n, carry):
        at = pl.ds(pl.multiple_of(n * 256, 256), 256)
        upat = pl.ds(pl.multiple_of(H + n * 256, 256), 256)
        a = dot(xrows[...], wgu[:, at])
        b = dot(xrows[...], wgu[:, upat])
        sig = jax.nn.sigmoid(a)
        act = a * sig
        h_s[:, at] = (act * b).astype(BF16)
        act_s[:, at] = act
        dact_s[:, at] = b * (sig * (1.0 + a * (1.0 - sig)))
        return carry

    lax.fori_loop(0, H // 256, forward, 0)
    swap = partials(0, lambda j: dot(h_s[...], wd[:, cols(j)]))
    swap.wait_recv()
    add_partials(0, 2)
    ex_z.begin()

    ex_dz.arrived()
    swap_dz = remote(zr.at[0], zr.at[1], 29, partner)
    start([swap_dz])
    swap_dz.wait_recv()
    unpack(zr, dzrows)

    def backward(n, carry):
        at = pl.ds(pl.multiple_of(n * 256, 256), 256)
        upat = pl.ds(pl.multiple_of(H + n * 256, 256), 256)
        dh = dot_cols(dzrows[...], wd[at, :])
        bg[:, at] = (dh * dact_s[:, at]).astype(BF16)
        bg[:, upat] = (dh * act_s[:, at]).astype(BF16)
        return carry

    lax.fori_loop(0, H // 256, backward, 0)

    def grads(p, carry):
        at = pl.ds(pl.multiple_of(p * 256, 256), 256)
        both = dot_rows(xrows[:, at], bg[...]).astype(BF16)
        down = dot_rows(dzrows[:, at], h_s[...]).astype(BF16)
        px, py = p // 2, (p % 2) * 2
        for i in range(2):
            rows = slice(i * 128, (i + 1) * 128)
            g_s[0, px, py + i] = both[rows, 0:Q]
            g_s[1, px, py + i] = both[rows, Q : 2 * Q]
            g_s[2, px, py + i, :, pl.ds(0, 256)] = both[rows, 2 * Q : 1024]
            g_s[2, px, py + i, :, pl.ds(256, 128)] = down[rows, 0:128]
            g_s[3, px, py + i] = down[rows, 128:512]
        return carry

    lax.fori_loop(0, 8, grads, 0)

    class Ring:
        def __init__(self, k, along_x, part, recv, out):
            self.recv, self.part, self.out = recv, part, out
            self.me = x if along_x else y
            base = 32 + 6 * k
            right, left = ring_dev(along_x, 1), ring_dev(along_x, -1)
            self.legs = [
                remote(part(0, self.at(2)), recv.at[0], base, right),
                remote(part(1, self.at(2)), recv.at[1], base + 1, left),
            ]
            self.direct = [
                remote(part(1, self.at(1)), recv.at[2], base + 2, right),
                remote(part(0, self.at(-1)), recv.at[3], base + 3, left),
            ]
            self.sums = [
                remote(out.at[0], recv.at[4], base + 4, right),
                remote(out.at[1], recv.at[5], base + 5, left),
            ]

        def at(self, d):
            return (self.me + d + 4) % 4

        def begin(self):
            start(self.legs)
            start(self.direct)

        def relay(self):
            for side, d in ((0, 1), (1, -1)):
                self.legs[side].wait_recv()
                mine = self.part(side, self.at(d))[...].astype(F32)
                self.out[side] = (mine + self.recv[side].astype(F32)).astype(BF16)
                start([self.sums[side]])

        def total(self, side):
            mine = self.part(side, self.me)[...].astype(F32)
            other = self.recv[3 - side].astype(F32)
            return mine + other + self.recv[4 + side].astype(F32)

        def arrived(self):
            for copy in self.direct + self.sums:
                copy.wait_recv()

    ring_a = [
        Ring(0, True, lambda s, p: g_s.at[s, p], a_recv.at[0], a_send.at[0]),
        Ring(1, False, lambda s, p: g_s.at[2 + s, :, p], a_recv.at[1], a_send.at[1]),
    ]
    ring_b = [
        Ring(2, False, lambda s, p: a_tot.at[0, s, p], b_recv.at[0], b_send.at[0]),
        Ring(3, True, lambda s, p: a_tot.at[1, s, p], b_recv.at[1], b_send.at[1]),
    ]
    for ring in ring_a:
        ring.begin()

    swap = partials(1, lambda j: dot_cols(bg[...], wgu[cols(j), :]))
    for ring in ring_a:
        ring.relay()
    swap.wait_recv()
    add_partials(1, 3)
    ex_dx.begin()

    def combine(j, carry):
        rows = back[:, main_rows(j), :].reshape(E * MAIN, W)
        value = dot_rows(gf[...], rows) + dot_rows(gfr[j], rest_of(back))
        mixed[:, cols(j)] = (value[0:T] + value[T:]).astype(BF16)
        return carry

    def store(src, dst, n):
        copy = pltpu.make_async_copy(src, dst, store_sem.at[n])
        copy.start()
        stores.append(copy)

    ex_z.arrived()
    lax.fori_loop(0, J, combine, 0)
    store(mixed, mixed_out, 2)

    for k, ring in enumerate(ring_a):
        ring.arrived()
        for side in range(2):
            a_tot[k, side] = ring.total(side).astype(BF16)
        ring_b[k].begin()
    for ring in ring_b:
        ring.relay()
    quarters = []
    for ring in ring_b:
        ring.arrived()
        quarters += [ring.total(0), ring.total(1)]
    q0, q1, q2, q3 = quarters
    grad_gate[:, pl.ds(0, Q)] = q0
    grad_gate[:, pl.ds(Q, H - Q)] = q1[:, 0:128]
    grad_up[:, pl.ds(0, 256)] = q1[:, 128:Q]
    grad_up[:, pl.ds(256, 256)] = q2[:, 0:256]
    grad_down[pl.ds(0, 128), :] = q2[:, 256:Q].T
    grad_down[pl.ds(128, Q), :] = q3.T

    store(grad_gate, grad_gate_out, 3)
    store(grad_up, grad_up_out, 4)
    store(grad_down, grad_down_out, 5)
    ex_dx.arrived()
    for copy in stores:
        copy.wait()
    for copy in started:
        copy.wait_send()


def finish(
    dx_in,
    left_in,
    left_rest_in,
    mixed_in,
    grad_gate_in,
    grad_up_in,
    grad_down_in,
    input_grad_out,
    mixed_out,
    grad_gate_out,
    grad_up_out,
    grad_down_out,
    dx,
    left,
    left_rest,
    input_grad,
    mixed,
    grad_gate,
    grad_up,
    grad_down,
    in_sem,
    out_sem,
):
    rest = pl.ds(J * MAIN, J * REM)
    masks = [
        pltpu.make_async_copy(left_in, left, in_sem.at[5]),
        pltpu.make_async_copy(left_rest_in, left_rest, in_sem.at[6]),
        pltpu.make_async_copy(dx_in.at[:, rest, :], dx.at[:, rest, :], in_sem.at[7]),
    ]
    pieces = []
    for j in range(J):
        rows = pl.ds(j * MAIN, MAIN)
        pieces.append(pltpu.make_async_copy(dx_in.at[:, rows, :], dx.at[:, rows, :], in_sem.at[j]))
    passed = [
        (mixed_in, mixed, mixed_out),
        (grad_gate_in, grad_gate, grad_gate_out),
        (grad_up_in, grad_up, grad_up_out),
        (grad_down_in, grad_down, grad_down_out),
    ]
    taken = [
        pltpu.make_async_copy(src, mid, in_sem.at[8 + n]) for n, (src, mid, _) in enumerate(passed)
    ]
    given = [
        pltpu.make_async_copy(mid, dst, out_sem.at[4 + n]) for n, (_, mid, dst) in enumerate(passed)
    ]
    for copy in masks + pieces + taken:
        copy.start()
    for take, give in zip(taken[0:1], given[0:1]):
        take.wait()
        give.start()
    for copy in masks:
        copy.wait()
    cut = dx[:, rest, :].reshape(E * J * REM, W)
    results = []
    for j in range(J):
        pieces[j].wait()
        rows = dx[:, pl.ds(j * MAIN, MAIN), :].reshape(E * MAIN, W)
        lanes = pl.ds(j * W, W)
        input_grad[:, lanes] = (dot(left[...], rows) + dot(left_rest[j], cut)).astype(BF16)
        result = pltpu.make_async_copy(
            input_grad.at[:, lanes], input_grad_out.at[:, lanes], out_sem.at[j]
        )
        result.start()
        results.append(result)
        if j + 1 < len(taken):
            taken[j + 1].wait()
            given[j + 1].start()
    for copy in given + results:
        copy.wait()


def per_device(tokens, routes, gates, cotangent, w_gate, w_up, w_down):
    vmem = pl.BlockSpec(memory_space=pltpu.VMEM)
    hbm = pl.BlockSpec(memory_space=pl.ANY)
    half = (4, 128, Q)
    outs = (
        jax.ShapeDtypeStruct((T, D), BF16),
        jax.ShapeDtypeStruct((128, H), F32),
        jax.ShapeDtypeStruct((128, H), F32),
        jax.ShapeDtypeStruct((H, 128), F32),
    )
    masks = (
        jax.ShapeDtypeStruct((E, BLK, W), BF16),
        jax.ShapeDtypeStruct((T, E * MAIN), BF16),
        jax.ShapeDtypeStruct((J, T, E * J * REM), BF16),
    )

    def held(shapes):
        return [pltpu.VMEM(s.shape, s.dtype) for s in shapes]

    mixed, dx_back, left, left_rest, gate, up, down = pl.pallas_call(
        kernel,
        out_shape=outs[0:1] + masks + outs[1:],
        in_specs=[vmem] * 2 + [hbm] * 5,
        out_specs=(hbm,) * 7,
        scratch_shapes=[
            pltpu.VMEM((T, D), BF16),
            pltpu.VMEM((T, D), BF16),
            *held(outs),
            *held(masks[1:]),
            pltpu.VMEM((D, 2 * H), BF16),
            pltpu.VMEM((H, D), BF16),
            pltpu.VMEM((E * MAIN, T), BF16),
            pltpu.VMEM((J, E * J * REM, T), BF16),
            pltpu.VMEM((E * MAIN, 2 * T), BF16),
            pltpu.VMEM((J, E * J * REM, 2 * T), BF16),
            pltpu.VMEM((J, E * REM, E * J * REM), BF16),
            pltpu.VMEM((4, E, BLK, W), BF16),
            pltpu.VMEM((2, E, BLK, W), BF16),
            pltpu.VMEM((2, E, BLK, W), BF16),
            pltpu.VMEM((E, BLK, W), BF16),
            pltpu.VMEM((ROWS, D), BF16),
            pltpu.VMEM((ROWS, D), BF16),
            pltpu.VMEM((ROWS, H), F32),
            pltpu.VMEM((ROWS, H), F32),
            pltpu.VMEM((ROWS, H), BF16),
            pltpu.VMEM((ROWS, 2 * H), BF16),
            pltpu.VMEM((E * (MAIN + REM), D), F32),
            pltpu.VMEM((2, E, BLK, W), BF16),
            pltpu.VMEM((2, E, BLK, W), BF16),
            pltpu.VMEM((4, 4, 4, 128, Q), BF16),
            pltpu.VMEM((2, 6) + half, BF16),
            pltpu.VMEM((2, 2) + half, BF16),
            pltpu.VMEM((2, 2) + half, BF16),
            pltpu.VMEM((2, 6, 128, Q), BF16),
            pltpu.VMEM((2, 2, 128, Q), BF16),
            pltpu.SemaphoreType.DMA((5,)),
            pltpu.SemaphoreType.DMA((6,)),
            pltpu.SemaphoreType.DMA((4,)),
            pltpu.SemaphoreType.DMA((56,)),
            pltpu.SemaphoreType.DMA((56,)),
        ],
        compiler_params=pltpu.CompilerParams(
            collective_id=0, has_side_effects=True, vmem_limit_bytes=63_000_000
        ),
        name="moe",
    )(routes.T, gates.T, tokens, cotangent, w_gate, w_up, w_down)
    input_grad, mixed, gate, up, down = pl.pallas_call(
        finish,
        out_shape=outs[0:1] + outs,
        in_specs=[hbm] * 7,
        out_specs=(hbm,) * 5,
        scratch_shapes=[
            *held(masks),
            *held(outs[0:1] + outs),
            pltpu.SemaphoreType.DMA((12,)),
            pltpu.SemaphoreType.DMA((8,)),
        ],
        compiler_params=pltpu.CompilerParams(vmem_limit_bytes=62_000_000),
        name="finish",
    )(dx_back, left, left_rest, mixed, gate, up, down)
    return mixed, input_grad, gate, up, down


def solution(mesh):
    in_specs = (
        P(("dp", "expert"), None),
        P(("dp", "expert"), None),
        P(("dp", "expert"), None),
        P(("dp", "expert"), None),
        P(None, "expert"),
        P(None, "expert"),
        P("expert", None),
    )
    out_specs = (
        P(("dp", "expert"), None),
        P(("dp", "expert"), None),
        P("dp", "expert"),
        P("dp", "expert"),
        P("expert", "dp"),
    )
    return jax.shard_map(
        per_device, mesh=mesh, in_specs=in_specs, out_specs=out_specs, check_vma=False
    )
```

```python
import jax
import jax.numpy as jnp
from jax import lax
from jax.experimental import pallas as pl
from jax.experimental.pallas import tpu as pltpu
from jax.sharding import PartitionSpec as P

MESH = pl.DeviceIdType.MESH
BF16 = jnp.bfloat16
F32 = jnp.float32

T = 128
D = 2048
H = 512
E = 8
MAIN = 32
REM = 4
W = 512
J = D // W
BLK = J * MAIN + J * REM
ROWS = 2 * E * (MAIN + REM)
Q = 384


def dot(a, b):
    return jnp.dot(a, b, preferred_element_type=F32)


def dot_rows(a, b):
    return lax.dot_general(a, b, (((0,), (0,)), ((), ())), preferred_element_type=F32)


def dot_cols(a, b):
    return lax.dot_general(a, b, (((1,), (1,)), ((), ())), preferred_element_type=F32)


def kernel(
    routes,
    gates,
    tokens_in,
    cotangent_in,
    w_gate,
    w_up,
    w_down,
    mixed_out,
    dx_back,
    left_out,
    left_rest_out,
    grad_gate_out,
    grad_up_out,
    grad_down_out,
    tokens,
    cotangent,
    mixed,
    grad_gate,
    grad_up,
    grad_down,
    left,
    left_rest,
    wgu,
    wd,
    gx,
    gxr,
    gf,
    gfr,
    perm,
    send,
    xr,
    zr,
    back,
    xrows,
    dzrows,
    act_s,
    dact_s,
    h_s,
    bg,
    own_s,
    part_out,
    part_in,
    g_s,
    a_recv,
    a_send,
    a_tot,
    b_recv,
    b_send,
    load_sem,
    store_sem,
    local_sem,
    ssem,
    rsem,
    ring_sem,
    near_sem,
):
    dp = lax.axis_index("dp")
    ex = lax.axis_index("expert")
    z, core = ex // 2, ex % 2
    x, y = dp // 4, dp % 4

    def zz(d):
        return (z + d + 8) % 8

    def zdev(d):
        return (dp, zz(d) * 2 + core)

    partner = (dp, z * 2 + (1 - core))

    def ring_dev(along_x, d):
        if along_x:
            return (((x + d + 4) % 4) * 4 + y, ex)
        return (x * 4 + (y + d + 4) % 4, ex)

    barrier = pltpu.get_barrier_semaphore()
    ring_peers = [zdev(d) for d in range(1, 8)]
    near = [partner, ring_dev(True, 1), ring_dev(True, -1), ring_dev(False, 1), ring_dev(False, -1)]
    first_member = z == 0

    def signal(sem, devices):
        for device in devices:
            pl.semaphore_signal(sem, inc=1, device_id=device, device_id_type=MESH)

    @pl.when(first_member)
    def _():
        signal(barrier, near)

    signal(barrier, ring_peers)

    load_x = pltpu.make_async_copy(tokens_in, tokens, load_sem.at[3])
    load_dy = pltpu.make_async_copy(cotangent_in, cotangent, load_sem.at[4])
    loads = [
        pltpu.make_async_copy(w_gate, wgu.at[:, pl.ds(0, H)], load_sem.at[0]),
        pltpu.make_async_copy(w_up, wgu.at[:, pl.ds(H, H)], load_sem.at[1]),
        pltpu.make_async_copy(w_down, wd, load_sem.at[2]),
    ]
    for load in [load_x, load_dy] + loads:
        load.start()

    row16 = lax.broadcasted_iota(jnp.int32, (16, T), 0)
    first = row16 == routes[0:1, :]
    second = row16 == routes[1:2, :]
    named = jnp.logical_or(first, second)
    earlier = lax.broadcasted_iota(jnp.int32, (T, T), 0) < lax.broadcasted_iota(jnp.int32, (T, T), 1)
    before = dot(
        jnp.where(named, 1.0, 0.0).astype(BF16), jnp.where(earlier, 1.0, 0.0).astype(BF16)
    ).astype(jnp.int32)
    slot = jnp.where(named, before, -1)
    gate = jnp.where(first, gates[0:1, :], 0) + jnp.where(second, gates[1:2, :], 0)
    high = ((gate >> 3) << 3).astype(F32) * (1.0 / 1024.0)
    low = (gate & 7).astype(F32) * (1.0 / 1024.0)
    rowm = lax.broadcasted_iota(jnp.int32, (MAIN, T), 0)
    rowr = lax.broadcasted_iota(jnp.int32, (J * REM, T), 0)
    def hits(e, j):
        if j is None:
            return rowm == slot[e : e + 1, :]
        hit = (MAIN + (rowr & (REM - 1))) == slot[e : e + 1, :]
        return jnp.logical_and(hit, (rowr >> 2) == j)

    for e in range(E):
        gx[pl.ds(e * MAIN, MAIN), :] = jnp.where(hits(e, None), 1.0, 0.0).astype(BF16)
        for j in range(J):
            rows = pl.ds(e * J * REM, J * REM)
            gxr[j, rows, :] = jnp.where(hits(e, j), 1.0, 0.0).astype(BF16)

    def scaled_masks():
        for e in range(E):
            for n, part in enumerate((high[e : e + 1, :], low[e : e + 1, :])):
                lanes = pl.ds(n * T, T)
                gf[pl.ds(e * MAIN, MAIN), lanes] = jnp.where(hits(e, None), part, 0.0).astype(BF16)
                for j in range(J):
                    rows = pl.ds(e * J * REM, J * REM)
                    gfr[j, rows, lanes] = jnp.where(hits(e, j), part, 0.0).astype(BF16)

    def other_masks():
        pr = lax.broadcasted_iota(jnp.int32, (E * REM, E * J * REM), 0)
        pc = lax.broadcasted_iota(jnp.int32, (E * REM, E * J * REM), 1)
        for j in range(J):
            same = jnp.logical_and(pr >> 2 == pc >> 4, (pc & 15) == j * REM + (pr & 3))
            perm[j] = jnp.where(same, 1.0, 0.0).astype(BF16)
            left_rest[j] = gxr[j].astype(F32).T.astype(BF16)
        left[...] = gx[...].astype(F32).T.astype(BF16)

    def cols(j):
        return pl.ds(pl.multiple_of(j * W, W), W)

    def main_rows(j):
        return pl.ds(pl.multiple_of(j * MAIN, MAIN), MAIN)

    def pack(buf, j, rows):
        buf[:, main_rows(j), :] = rows.reshape(E, MAIN, W)

    def pack_rest(buf, rest):
        buf[:, pl.ds(J * MAIN, J * REM), :] = rest.astype(BF16).reshape(E, J * REM, W)

    def rest_of(buf):
        return buf[:, pl.ds(J * MAIN, J * REM), :].reshape(E * J * REM, W)

    def gather_x(j, rest):
        piece = tokens[:, cols(j)]
        pack(send.at[0], j, dot(gx[...], piece).astype(BF16))
        return rest + dot(gxr[j], piece)

    def gather_dz(j, rest):
        piece = cotangent[:, cols(j)]
        both = jnp.concatenate([piece, piece], axis=0)
        pack(send.at[1], j, dot(gf[...], both).astype(BF16))
        return rest + dot(gfr[j], both)

    zero_rest = jnp.zeros((E * J * REM, W), F32)

    def remote(src, dst, index, device):
        return pltpu.make_async_remote_copy(
            src_ref=src,
            dst_ref=dst,
            send_sem=ssem.at[index],
            recv_sem=rsem.at[index],
            device_id=device,
            device_id_type=MESH,
        )

    started = []

    def start(copies):
        for copy in copies:
            copy.start()
            started.append(copy)

    class Exchange:
        def __init__(self, k, recv):
            src = send.at[k]
            self.copies = [
                remote(src.at[zz(d)], recv.at[z], 7 * k + n, zdev(d))
                for n, d in enumerate((4, 3, -3, 2, -2, 1, -1))
            ]
            self.own = pltpu.make_async_copy(src.at[z], recv.at[z], local_sem.at[k])

        def begin(self):
            start(self.copies)
            self.own.start()

        def arrived(self):
            for copy in self.copies:
                copy.wait_recv()
            self.own.wait()

    def unpack(got, rows):
        for g in range(2):

            def one(j, carry):
                rows[pl.ds(g * E * MAIN, E * MAIN), cols(j)] = got[g, :, main_rows(j), :].reshape(
                    E * MAIN, W
                )
                rest = dot(perm[j], rest_of(got.at[g])).astype(BF16)
                rows[pl.ds(2 * E * MAIN + g * E * REM, E * REM), cols(j)] = rest
                return carry

            lax.fori_loop(0, J, one, 0)

    om, orr = pl.ds(0, E * MAIN), pl.ds(E * MAIN, E * REM)

    def partials(k, product):
        def one(j, rest):
            value = product(j)
            n = E * MAIN
            pack(part_out.at[k], j, value[n : 2 * n].astype(BF16))
            own_s[om, cols(j)] = value[0:n]
            own_s[orr, cols(j)] = value[2 * n : 2 * n + E * REM]
            return rest + dot_rows(perm[j], value[2 * n + E * REM :].astype(BF16))

        pack_rest(part_out.at[k], lax.fori_loop(0, J, one, zero_rest))
        swap = remote(part_out.at[k], part_in.at[k], 30 + k, partner)
        start([swap])
        return swap

    def add_partials(k, to):
        def one(j, rest):
            got = part_in[k, :, main_rows(j), :].reshape(E * MAIN, W).astype(F32)
            pack(send.at[to], j, (own_s[om, cols(j)] + got).astype(BF16))
            more = own_s[orr, cols(j)] + dot(perm[j], rest_of(part_in.at[k]))
            return rest + dot_rows(perm[j], more.astype(BF16))

        pack_rest(send.at[to], lax.fori_loop(0, J, one, zero_rest))

    ex_x, ex_dz = Exchange(0, xr.at[0]), Exchange(1, zr.at[0])
    ex_z, ex_dx = Exchange(2, back), Exchange(3, dx_back)

    load_x.wait()
    pack_rest(send.at[0], lax.fori_loop(0, J, gather_x, zero_rest))

    @pl.when(jnp.logical_not(first_member))
    def _():
        pl.semaphore_wait(barrier, len(ring_peers))

    @pl.when(first_member)
    def _():
        pl.semaphore_wait(barrier, len(ring_peers) + len(near))
        signal(ring_sem, near)

    ex_x.begin()
    scaled_masks()
    load_dy.wait()
    pack_rest(send.at[1], lax.fori_loop(0, J, gather_dz, zero_rest))
    ex_dz.begin()
    other_masks()
    stores = [
        pltpu.make_async_copy(left, left_out, store_sem.at[0]),
        pltpu.make_async_copy(left_rest, left_rest_out, store_sem.at[1]),
    ]
    for store in stores:
        store.start()

    @pl.when(first_member)
    def _():
        pl.semaphore_wait(ring_sem, len(near))
        signal(near_sem, ring_peers)

    ex_x.arrived()

    @pl.when(jnp.logical_not(first_member))
    def _():
        pl.semaphore_wait(near_sem, 1)

    swap_x = remote(xr.at[0], xr.at[1], 28, partner)
    start([swap_x])
    for load in loads:
        load.wait()
    swap_x.wait_recv()

    unpack(xr, xrows)

    def forward(n, carry):
        at = pl.ds(pl.multiple_of(n * 256, 256), 256)
        upat = pl.ds(pl.multiple_of(H + n * 256, 256), 256)
        a = dot(xrows[...], wgu[:, at])
        b = dot(xrows[...], wgu[:, upat])
        sig = jax.nn.sigmoid(a)
        act = a * sig
        h_s[:, at] = (act * b).astype(BF16)
        act_s[:, at] = act
        dact_s[:, at] = b * (sig * (1.0 + a * (1.0 - sig)))
        return carry

    lax.fori_loop(0, H // 256, forward, 0)
    swap = partials(0, lambda j: dot(h_s[...], wd[:, cols(j)]))
    swap.wait_recv()
    add_partials(0, 2)
    ex_z.begin()

    ex_dz.arrived()
    swap_dz = remote(zr.at[0], zr.at[1], 29, partner)
    start([swap_dz])
    swap_dz.wait_recv()
    unpack(zr, dzrows)

    def backward(n, carry):
        at = pl.ds(pl.multiple_of(n * 256, 256), 256)
        upat = pl.ds(pl.multiple_of(H + n * 256, 256), 256)
        dh = dot_cols(dzrows[...], wd[at, :])
        bg[:, at] = (dh * dact_s[:, at]).astype(BF16)
        bg[:, upat] = (dh * act_s[:, at]).astype(BF16)
        return carry

    lax.fori_loop(0, H // 256, backward, 0)

    def grads(p, carry):
        at = pl.ds(pl.multiple_of(p * 256, 256), 256)
        both = dot_rows(xrows[:, at], bg[...]).astype(BF16)
        down = dot_rows(dzrows[:, at], h_s[...]).astype(BF16)
        px, py = p // 2, (p % 2) * 2
        for i in range(2):
            rows = slice(i * 128, (i + 1) * 128)
            g_s[0, px, py + i] = both[rows, 0:Q]
            g_s[1, px, py + i] = both[rows, Q : 2 * Q]
            g_s[2, px, py + i, :, pl.ds(0, 256)] = both[rows, 2 * Q : 1024]
            g_s[2, px, py + i, :, pl.ds(256, 128)] = down[rows, 0:128]
            g_s[3, px, py + i] = down[rows, 128:512]
        return carry

    lax.fori_loop(0, 8, grads, 0)

    class Ring:
        def __init__(self, k, along_x, part, recv, out):
            self.recv, self.part, self.out = recv, part, out
            self.me = x if along_x else y
            base = 32 + 6 * k
            right, left = ring_dev(along_x, 1), ring_dev(along_x, -1)
            self.legs = [
                remote(part(0, self.at(2)), recv.at[0], base, right),
                remote(part(1, self.at(2)), recv.at[1], base + 1, left),
            ]
            self.direct = [
                remote(part(1, self.at(1)), recv.at[2], base + 2, right),
                remote(part(0, self.at(-1)), recv.at[3], base + 3, left),
            ]
            self.sums = [
                remote(out.at[0], recv.at[4], base + 4, right),
                remote(out.at[1], recv.at[5], base + 5, left),
            ]

        def at(self, d):
            return (self.me + d + 4) % 4

        def begin(self):
            start(self.legs)
            start(self.direct)

        def relay(self):
            for side, d in ((0, 1), (1, -1)):
                self.legs[side].wait_recv()
                mine = self.part(side, self.at(d))[...].astype(F32)
                self.out[side] = (mine + self.recv[side].astype(F32)).astype(BF16)
                start([self.sums[side]])

        def total(self, side):
            mine = self.part(side, self.me)[...].astype(F32)
            other = self.recv[3 - side].astype(F32)
            return mine + other + self.recv[4 + side].astype(F32)

        def arrived(self):
            for copy in self.direct + self.sums:
                copy.wait_recv()

    ring_a = [
        Ring(0, True, lambda s, p: g_s.at[s, p], a_recv.at[0], a_send.at[0]),
        Ring(1, False, lambda s, p: g_s.at[2 + s, :, p], a_recv.at[1], a_send.at[1]),
    ]
    ring_b = [
        Ring(2, False, lambda s, p: a_tot.at[0, s, p], b_recv.at[0], b_send.at[0]),
        Ring(3, True, lambda s, p: a_tot.at[1, s, p], b_recv.at[1], b_send.at[1]),
    ]
    for ring in ring_a:
        ring.begin()

    swap = partials(1, lambda j: dot_cols(bg[...], wgu[cols(j), :]))
    for ring in ring_a:
        ring.relay()
    swap.wait_recv()
    add_partials(1, 3)
    ex_dx.begin()

    def combine(j, carry):
        rows = back[:, main_rows(j), :].reshape(E * MAIN, W)
        value = dot_rows(gf[...], rows) + dot_rows(gfr[j], rest_of(back))
        mixed[:, cols(j)] = (value[0:T] + value[T:]).astype(BF16)
        return carry

    def store(src, dst, n):
        copy = pltpu.make_async_copy(src, dst, store_sem.at[n])
        copy.start()
        stores.append(copy)

    ex_z.arrived()
    lax.fori_loop(0, J, combine, 0)
    store(mixed, mixed_out, 2)

    for k, ring in enumerate(ring_a):
        ring.arrived()
        for side in range(2):
            a_tot[k, side] = ring.total(side).astype(BF16)
        ring_b[k].begin()
    for ring in ring_b:
        ring.relay()
    quarters = []
    for ring in ring_b:
        ring.arrived()
        quarters += [ring.total(0), ring.total(1)]
    q0, q1, q2, q3 = quarters
    grad_gate[:, pl.ds(0, Q)] = q0
    grad_gate[:, pl.ds(Q, H - Q)] = q1[:, 0:128]
    grad_up[:, pl.ds(0, 256)] = q1[:, 128:Q]
    grad_up[:, pl.ds(256, 256)] = q2[:, 0:256]
    grad_down[pl.ds(0, 128), :] = q2[:, 256:Q].T
    grad_down[pl.ds(128, Q), :] = q3.T

    store(grad_gate, grad_gate_out, 3)
    store(grad_up, grad_up_out, 4)
    store(grad_down, grad_down_out, 5)
    ex_dx.arrived()
    for copy in stores:
        copy.wait()
    for copy in started:
        copy.wait_send()


def finish(
    dx_in,
    left_in,
    left_rest_in,
    mixed_in,
    grad_gate_in,
    grad_up_in,
    grad_down_in,
    input_grad_out,
    mixed_out,
    grad_gate_out,
    grad_up_out,
    grad_down_out,
    dx,
    left,
    left_rest,
    input_grad,
    mixed,
    grad_gate,
    grad_up,
    grad_down,
    in_sem,
    out_sem,
):
    rest = pl.ds(J * MAIN, J * REM)
    masks = [
        pltpu.make_async_copy(left_in, left, in_sem.at[5]),
        pltpu.make_async_copy(left_rest_in, left_rest, in_sem.at[6]),
        pltpu.make_async_copy(dx_in.at[:, rest, :], dx.at[:, rest, :], in_sem.at[7]),
    ]
    pieces = []
    for j in range(J):
        rows = pl.ds(j * MAIN, MAIN)
        pieces.append(pltpu.make_async_copy(dx_in.at[:, rows, :], dx.at[:, rows, :], in_sem.at[j]))
    passed = [
        (mixed_in, mixed, mixed_out),
        (grad_gate_in, grad_gate, grad_gate_out),
        (grad_up_in, grad_up, grad_up_out),
        (grad_down_in, grad_down, grad_down_out),
    ]
    taken = [
        pltpu.make_async_copy(src, mid, in_sem.at[8 + n]) for n, (src, mid, _) in enumerate(passed)
    ]
    given = [
        pltpu.make_async_copy(mid, dst, out_sem.at[4 + n]) for n, (_, mid, dst) in enumerate(passed)
    ]
    for copy in masks + pieces + taken:
        copy.start()
    for take, give in zip(taken[0:1], given[0:1]):
        take.wait()
        give.start()
    for copy in masks:
        copy.wait()
    cut = dx[:, rest, :].reshape(E * J * REM, W)
    results = []
    for j in range(J):
        pieces[j].wait()
        rows = dx[:, pl.ds(j * MAIN, MAIN), :].reshape(E * MAIN, W)
        lanes = pl.ds(j * W, W)
        input_grad[:, lanes] = (dot(left[...], rows) + dot(left_rest[j], cut)).astype(BF16)
        result = pltpu.make_async_copy(
            input_grad.at[:, lanes], input_grad_out.at[:, lanes], out_sem.at[j]
        )
        result.start()
        results.append(result)
        if j + 1 < len(taken):
            taken[j + 1].wait()
            given[j + 1].start()
    for copy in given + results:
        copy.wait()


def per_device(tokens, routes, gates, cotangent, w_gate, w_up, w_down):
    vmem = pl.BlockSpec(memory_space=pltpu.VMEM)
    hbm = pl.BlockSpec(memory_space=pl.ANY)
    half = (4, 128, Q)
    outs = (
        jax.ShapeDtypeStruct((T, D), BF16),
        jax.ShapeDtypeStruct((128, H), F32),
        jax.ShapeDtypeStruct((128, H), F32),
        jax.ShapeDtypeStruct((H, 128), F32),
    )
    masks = (
        jax.ShapeDtypeStruct((E, BLK, W), BF16),
        jax.ShapeDtypeStruct((T, E * MAIN), BF16),
        jax.ShapeDtypeStruct((J, T, E * J * REM), BF16),
    )

    def held(shapes):
        return [pltpu.VMEM(s.shape, s.dtype) for s in shapes]

    mixed, dx_back, left, left_rest, gate, up, down = pl.pallas_call(
        kernel,
        out_shape=outs[0:1] + masks + outs[1:],
        in_specs=[vmem] * 2 + [hbm] * 5,
        out_specs=(hbm,) * 7,
        scratch_shapes=[
            pltpu.VMEM((T, D), BF16),
            pltpu.VMEM((T, D), BF16),
            *held(outs),
            *held(masks[1:]),
            pltpu.VMEM((D, 2 * H), BF16),
            pltpu.VMEM((H, D), BF16),
            pltpu.VMEM((E * MAIN, T), BF16),
            pltpu.VMEM((J, E * J * REM, T), BF16),
            pltpu.VMEM((E * MAIN, 2 * T), BF16),
            pltpu.VMEM((J, E * J * REM, 2 * T), BF16),
            pltpu.VMEM((J, E * REM, E * J * REM), BF16),
            pltpu.VMEM((4, E, BLK, W), BF16),
            pltpu.VMEM((2, E, BLK, W), BF16),
            pltpu.VMEM((2, E, BLK, W), BF16),
            pltpu.VMEM((E, BLK, W), BF16),
            pltpu.VMEM((ROWS, D), BF16),
            pltpu.VMEM((ROWS, D), BF16),
            pltpu.VMEM((ROWS, H), F32),
            pltpu.VMEM((ROWS, H), F32),
            pltpu.VMEM((ROWS, H), BF16),
            pltpu.VMEM((ROWS, 2 * H), BF16),
            pltpu.VMEM((E * (MAIN + REM), D), F32),
            pltpu.VMEM((2, E, BLK, W), BF16),
            pltpu.VMEM((2, E, BLK, W), BF16),
            pltpu.VMEM((4, 4, 4, 128, Q), BF16),
            pltpu.VMEM((2, 6) + half, BF16),
            pltpu.VMEM((2, 2) + half, BF16),
            pltpu.VMEM((2, 2) + half, BF16),
            pltpu.VMEM((2, 6, 128, Q), BF16),
            pltpu.VMEM((2, 2, 128, Q), BF16),
            pltpu.SemaphoreType.DMA((5,)),
            pltpu.SemaphoreType.DMA((6,)),
            pltpu.SemaphoreType.DMA((4,)),
            pltpu.SemaphoreType.DMA((56,)),
            pltpu.SemaphoreType.DMA((56,)),
            pltpu.SemaphoreType.REGULAR,
            pltpu.SemaphoreType.REGULAR,
        ],
        compiler_params=pltpu.CompilerParams(
            collective_id=0, has_side_effects=True, vmem_limit_bytes=63_000_000
        ),
        name="moe",
    )(routes.T, gates.T, tokens, cotangent, w_gate, w_up, w_down)
    input_grad, mixed, gate, up, down = pl.pallas_call(
        finish,
        out_shape=outs[0:1] + outs,
        in_specs=[hbm] * 7,
        out_specs=(hbm,) * 5,
        scratch_shapes=[
            *held(masks),
            *held(outs[0:1] + outs),
            pltpu.SemaphoreType.DMA((12,)),
            pltpu.SemaphoreType.DMA((8,)),
        ],
        compiler_params=pltpu.CompilerParams(vmem_limit_bytes=62_000_000),
        name="finish",
    )(dx_back, left, left_rest, mixed, gate, up, down)
    return mixed, input_grad, gate, up, down


def solution(mesh):
    in_specs = (
        P(("dp", "expert"), None),
        P(("dp", "expert"), None),
        P(("dp", "expert"), None),
        P(("dp", "expert"), None),
        P(None, "expert"),
        P(None, "expert"),
        P("expert", None),
    )
    out_specs = (
        P(("dp", "expert"), None),
        P(("dp", "expert"), None),
        P("dp", "expert"),
        P("dp", "expert"),
        P("expert", "dp"),
    )
    return jax.shard_map(
        per_device, mesh=mesh, in_specs=in_specs, out_specs=out_specs, check_vma=False
    )
```

```python
import jax
import jax.numpy as jnp
from jax import lax
from jax.experimental import pallas as pl
from jax.experimental.pallas import tpu as pltpu
from jax.sharding import PartitionSpec as P

MESH = pl.DeviceIdType.MESH
BF16 = jnp.bfloat16
F32 = jnp.float32

T = 128
D = 2048
H = 512
E = 8
MAIN = 32
REM = 4
W = 512
J = D // W
BLK = J * MAIN + J * REM
ROWS = 2 * E * (MAIN + REM)
Q = 384


def dot(a, b):
    return jnp.dot(a, b, preferred_element_type=F32)


def dot_rows(a, b):
    return lax.dot_general(a, b, (((0,), (0,)), ((), ())), preferred_element_type=F32)


def dot_cols(a, b):
    return lax.dot_general(a, b, (((1,), (1,)), ((), ())), preferred_element_type=F32)


def kernel(
    routes,
    gates,
    tokens_in,
    cotangent_in,
    w_gate,
    w_up,
    w_down,
    mixed_out,
    dx_back,
    left_out,
    left_rest_out,
    grad_gate_out,
    grad_up_out,
    grad_down_out,
    tokens,
    cotangent,
    mixed,
    grad_gate,
    grad_up,
    grad_down,
    left,
    left_rest,
    wgu,
    wd,
    gx,
    gxr,
    gf,
    gfr,
    perm,
    send,
    xr,
    zr,
    back,
    xrows,
    dzrows,
    act_s,
    dact_s,
    h_s,
    bg,
    own_s,
    part_out,
    part_in,
    g_s,
    a_recv,
    a_send,
    a_tot,
    b_recv,
    b_send,
    load_sem,
    store_sem,
    local_sem,
    ssem,
    rsem,
    ring_sem,
    near_sem,
):
    dp = lax.axis_index("dp")
    ex = lax.axis_index("expert")
    z, core = ex // 2, ex % 2
    x, y = dp // 4, dp % 4

    def zz(d):
        return (z + d + 8) % 8

    def zdev(d):
        return (dp, zz(d) * 2 + core)

    partner = (dp, z * 2 + (1 - core))

    def ring_dev(along_x, d):
        if along_x:
            return (((x + d + 4) % 4) * 4 + y, ex)
        return (x * 4 + (y + d + 4) % 4, ex)

    barrier = pltpu.get_barrier_semaphore()
    ring_peers = [zdev(d) for d in range(1, 8)]
    near = [partner, ring_dev(True, 1), ring_dev(True, -1), ring_dev(False, 1), ring_dev(False, -1)]
    first_member = z == 0

    def signal(sem, devices):
        for device in devices:
            pl.semaphore_signal(sem, inc=1, device_id=device, device_id_type=MESH)

    @pl.when(first_member)
    def _():
        signal(barrier, near)

    signal(barrier, ring_peers)

    load_x = pltpu.make_async_copy(tokens_in, tokens, load_sem.at[3])
    load_dy = pltpu.make_async_copy(cotangent_in, cotangent, load_sem.at[4])
    loads = [
        pltpu.make_async_copy(w_gate, wgu.at[:, pl.ds(0, H)], load_sem.at[0]),
        pltpu.make_async_copy(w_up, wgu.at[:, pl.ds(H, H)], load_sem.at[1]),
        pltpu.make_async_copy(w_down, wd, load_sem.at[2]),
    ]
    for load in [load_x, load_dy] + loads:
        load.start()

    row16 = lax.broadcasted_iota(jnp.int32, (16, T), 0)
    first = row16 == routes[0:1, :]
    second = row16 == routes[1:2, :]
    named = jnp.logical_or(first, second)
    earlier = lax.broadcasted_iota(jnp.int32, (T, T), 0) < lax.broadcasted_iota(jnp.int32, (T, T), 1)
    before = dot(
        jnp.where(named, 1.0, 0.0).astype(BF16), jnp.where(earlier, 1.0, 0.0).astype(BF16)
    ).astype(jnp.int32)
    slot = jnp.where(named, before, -1)
    gate = jnp.where(first, gates[0:1, :], 0) + jnp.where(second, gates[1:2, :], 0)
    high = ((gate >> 3) << 3).astype(F32) * (1.0 / 1024.0)
    low = (gate & 7).astype(F32) * (1.0 / 1024.0)
    rowm = lax.broadcasted_iota(jnp.int32, (MAIN, T), 0)
    rowr = lax.broadcasted_iota(jnp.int32, (J * REM, T), 0)
    def hits(e, j):
        if j is None:
            return rowm == slot[e : e + 1, :]
        hit = (MAIN + (rowr & (REM - 1))) == slot[e : e + 1, :]
        return jnp.logical_and(hit, (rowr >> 2) == j)

    for e in range(E):
        gx[pl.ds(e * MAIN, MAIN), :] = jnp.where(hits(e, None), 1.0, 0.0).astype(BF16)
        for j in range(J):
            rows = pl.ds(e * J * REM, J * REM)
            gxr[j, rows, :] = jnp.where(hits(e, j), 1.0, 0.0).astype(BF16)

    def scaled_masks():
        for e in range(E):
            for n, part in enumerate((high[e : e + 1, :], low[e : e + 1, :])):
                lanes = pl.ds(n * T, T)
                gf[pl.ds(e * MAIN, MAIN), lanes] = jnp.where(hits(e, None), part, 0.0).astype(BF16)
                for j in range(J):
                    rows = pl.ds(e * J * REM, J * REM)
                    gfr[j, rows, lanes] = jnp.where(hits(e, j), part, 0.0).astype(BF16)

    def other_masks():
        pr = lax.broadcasted_iota(jnp.int32, (E * REM, E * J * REM), 0)
        pc = lax.broadcasted_iota(jnp.int32, (E * REM, E * J * REM), 1)
        for j in range(J):
            same = jnp.logical_and(pr >> 2 == pc >> 4, (pc & 15) == j * REM + (pr & 3))
            perm[j] = jnp.where(same, 1.0, 0.0).astype(BF16)
            left_rest[j] = gxr[j].astype(F32).T.astype(BF16)
        left[...] = gx[...].astype(F32).T.astype(BF16)

    def cols(j):
        return pl.ds(pl.multiple_of(j * W, W), W)

    def main_rows(j):
        return pl.ds(pl.multiple_of(j * MAIN, MAIN), MAIN)

    def pack(buf, j, rows):
        buf[:, main_rows(j), :] = rows.reshape(E, MAIN, W)

    def pack_rest(buf, rest):
        buf[:, pl.ds(J * MAIN, J * REM), :] = rest.astype(BF16).reshape(E, J * REM, W)

    def rest_of(buf):
        return buf[:, pl.ds(J * MAIN, J * REM), :].reshape(E * J * REM, W)

    def gather_x(j, rest):
        piece = tokens[:, cols(j)]
        pack(send.at[0], j, dot(gx[...], piece).astype(BF16))
        return rest + dot(gxr[j], piece)

    def gather_dz(j, rest):
        piece = cotangent[:, cols(j)]
        both = jnp.concatenate([piece, piece], axis=0)
        pack(send.at[1], j, dot(gf[...], both).astype(BF16))
        return rest + dot(gfr[j], both)

    zero_rest = jnp.zeros((E * J * REM, W), F32)

    def remote(src, dst, index, device):
        return pltpu.make_async_remote_copy(
            src_ref=src,
            dst_ref=dst,
            send_sem=ssem.at[index],
            recv_sem=rsem.at[index],
            device_id=device,
            device_id_type=MESH,
        )

    started = []

    def start(copies):
        for copy in copies:
            copy.start()
            started.append(copy)

    class Exchange:
        def __init__(self, k, recv):
            src = send.at[k]
            self.copies = [
                remote(src.at[zz(d)], recv.at[z], 7 * k + n, zdev(d))
                for n, d in enumerate((4, 3, -3, 2, -2, 1, -1))
            ]
            self.own = pltpu.make_async_copy(src.at[z], recv.at[z], local_sem.at[k])

        def begin(self):
            start(self.copies)
            self.own.start()

        def arrived(self):
            for copy in self.copies:
                copy.wait_recv()
            self.own.wait()

    def unpack(got, rows):
        for g in range(2):

            def one(j, carry):
                rows[pl.ds(g * E * MAIN, E * MAIN), cols(j)] = got[g, :, main_rows(j), :].reshape(
                    E * MAIN, W
                )
                rest = dot(perm[j], rest_of(got.at[g])).astype(BF16)
                rows[pl.ds(2 * E * MAIN + g * E * REM, E * REM), cols(j)] = rest
                return carry

            lax.fori_loop(0, J, one, 0)

    om, orr = pl.ds(0, E * MAIN), pl.ds(E * MAIN, E * REM)

    def partials(k, product):
        def one(j, rest):
            value = product(j)
            n = E * MAIN
            pack(part_out.at[k], j, value[n : 2 * n].astype(BF16))
            own_s[om, cols(j)] = value[0:n]
            own_s[orr, cols(j)] = value[2 * n : 2 * n + E * REM]
            return rest + dot_rows(perm[j], value[2 * n + E * REM :].astype(BF16))

        pack_rest(part_out.at[k], lax.fori_loop(0, J, one, zero_rest))
        swap = remote(part_out.at[k], part_in.at[k], 30 + k, partner)
        start([swap])
        return swap

    def add_partials(k, to):
        def one(j, rest):
            got = part_in[k, :, main_rows(j), :].reshape(E * MAIN, W).astype(F32)
            pack(send.at[to], j, (own_s[om, cols(j)] + got).astype(BF16))
            more = own_s[orr, cols(j)] + dot(perm[j], rest_of(part_in.at[k]))
            return rest + dot_rows(perm[j], more.astype(BF16))

        pack_rest(send.at[to], lax.fori_loop(0, J, one, zero_rest))

    ex_x, ex_dz = Exchange(0, xr.at[0]), Exchange(1, zr.at[0])
    ex_z, ex_dx = Exchange(2, back), Exchange(3, dx_back)

    load_x.wait()
    pack_rest(send.at[0], lax.fori_loop(0, J, gather_x, zero_rest))

    @pl.when(jnp.logical_not(first_member))
    def _():
        pl.semaphore_wait(barrier, len(ring_peers))

    @pl.when(first_member)
    def _():
        pl.semaphore_wait(barrier, len(ring_peers) + len(near))
        signal(ring_sem, near)

    ex_x.begin()
    scaled_masks()
    load_dy.wait()
    pack_rest(send.at[1], lax.fori_loop(0, J, gather_dz, zero_rest))
    ex_dz.begin()
    other_masks()
    stores = [
        pltpu.make_async_copy(left, left_out, store_sem.at[0]),
        pltpu.make_async_copy(left_rest, left_rest_out, store_sem.at[1]),
    ]
    for store in stores:
        store.start()

    @pl.when(first_member)
    def _():
        pl.semaphore_wait(ring_sem, len(near))
        signal(near_sem, ring_peers)

    ex_x.arrived()

    @pl.when(jnp.logical_not(first_member))
    def _():
        pl.semaphore_wait(near_sem, 1)

    swap_x = remote(xr.at[0], xr.at[1], 28, partner)
    start([swap_x])
    for load in loads:
        load.wait()
    swap_x.wait_recv()

    unpack(xr, xrows)

    def forward(n, carry):
        at = pl.ds(pl.multiple_of(n * 256, 256), 256)
        upat = pl.ds(pl.multiple_of(H + n * 256, 256), 256)
        a = dot(xrows[...], wgu[:, at])
        b = dot(xrows[...], wgu[:, upat])
        sig = jax.nn.sigmoid(a)
        act = a * sig
        h_s[:, at] = (act * b).astype(BF16)
        act_s[:, at] = act
        dact_s[:, at] = b * (sig * (1.0 + a * (1.0 - sig)))
        return carry

    lax.fori_loop(0, H // 256, forward, 0)
    swap = partials(0, lambda j: dot(h_s[...], wd[:, cols(j)]))
    swap.wait_recv()
    add_partials(0, 2)
    ex_z.begin()

    ex_dz.arrived()
    swap_dz = remote(zr.at[0], zr.at[1], 29, partner)
    start([swap_dz])
    swap_dz.wait_recv()
    unpack(zr, dzrows)

    def backward(n, carry):
        at = pl.ds(pl.multiple_of(n * 256, 256), 256)
        upat = pl.ds(pl.multiple_of(H + n * 256, 256), 256)
        dh = dot_cols(dzrows[...], wd[at, :])
        bg[:, at] = (dh * dact_s[:, at]).astype(BF16)
        bg[:, upat] = (dh * act_s[:, at]).astype(BF16)
        return carry

    lax.fori_loop(0, H // 256, backward, 0)

    def grads(p, carry):
        at = pl.ds(pl.multiple_of(p * 256, 256), 256)
        both = dot_rows(xrows[:, at], bg[...]).astype(BF16)
        down = dot_rows(dzrows[:, at], h_s[...]).astype(BF16)
        px, py = p // 2, (p % 2) * 2
        for i in range(2):
            rows = slice(i * 128, (i + 1) * 128)
            g_s[0, px, py + i] = both[rows, 0:Q]
            g_s[1, px, py + i] = both[rows, Q : 2 * Q]
            g_s[2, px, py + i, :, pl.ds(0, 256)] = both[rows, 2 * Q : 1024]
            g_s[2, px, py + i, :, pl.ds(256, 128)] = down[rows, 0:128]
            g_s[3, px, py + i] = down[rows, 128:512]
        return carry

    lax.fori_loop(0, 8, grads, 0)

    class Ring:
        def __init__(self, k, along_x, part, recv, out):
            self.recv, self.part, self.out = recv, part, out
            self.me = x if along_x else y
            base = 32 + 6 * k
            right, left = ring_dev(along_x, 1), ring_dev(along_x, -1)
            self.legs = [
                remote(part(0, self.at(2)), recv.at[0], base, right),
                remote(part(1, self.at(2)), recv.at[1], base + 1, left),
            ]
            self.direct = [
                remote(part(1, self.at(1)), recv.at[2], base + 2, right),
                remote(part(0, self.at(-1)), recv.at[3], base + 3, left),
            ]
            self.sums = [
                remote(out.at[0], recv.at[4], base + 4, right),
                remote(out.at[1], recv.at[5], base + 5, left),
            ]

        def at(self, d):
            return (self.me + d + 4) % 4

        def begin(self):
            start(self.legs)
            start(self.direct)

        def relay(self):
            for side, d in ((0, 1), (1, -1)):
                self.legs[side].wait_recv()
                mine = self.part(side, self.at(d))[...].astype(F32)
                self.out[side] = (mine + self.recv[side].astype(F32)).astype(BF16)
                start([self.sums[side]])

        def total(self, side):
            mine = self.part(side, self.me)[...].astype(F32)
            other = self.recv[3 - side].astype(F32)
            return mine + other + self.recv[4 + side].astype(F32)

        def arrived(self):
            for copy in self.direct + self.sums:
                copy.wait_recv()

    ring_a = [
        Ring(0, True, lambda s, p: g_s.at[s, p], a_recv.at[0], a_send.at[0]),
        Ring(1, False, lambda s, p: g_s.at[2 + s, :, p], a_recv.at[1], a_send.at[1]),
    ]
    ring_b = [
        Ring(2, False, lambda s, p: a_tot.at[0, s, p], b_recv.at[0], b_send.at[0]),
        Ring(3, True, lambda s, p: a_tot.at[1, s, p], b_recv.at[1], b_send.at[1]),
    ]
    for ring in ring_a:
        ring.begin()

    swap = partials(1, lambda j: dot_cols(bg[...], wgu[cols(j), :]))
    swap.wait_recv()
    add_partials(1, 3)
    ex_dx.begin()
    for ring in ring_a:
        ring.relay()

    def combine(j, carry):
        rows = back[:, main_rows(j), :].reshape(E * MAIN, W)
        value = dot_rows(gf[...], rows) + dot_rows(gfr[j], rest_of(back))
        mixed[:, cols(j)] = (value[0:T] + value[T:]).astype(BF16)
        return carry

    def store(src, dst, n):
        copy = pltpu.make_async_copy(src, dst, store_sem.at[n])
        copy.start()
        stores.append(copy)

    ex_z.arrived()
    lax.fori_loop(0, J, combine, 0)
    store(mixed, mixed_out, 2)

    for k, ring in enumerate(ring_a):
        ring.arrived()
        for side in range(2):
            a_tot[k, side] = ring.total(side).astype(BF16)
        ring_b[k].begin()
    for ring in ring_b:
        ring.relay()
    quarters = []
    for ring in ring_b:
        ring.arrived()
        quarters += [ring.total(0), ring.total(1)]
    q0, q1, q2, q3 = quarters
    grad_gate[:, pl.ds(0, Q)] = q0
    grad_gate[:, pl.ds(Q, H - Q)] = q1[:, 0:128]
    grad_up[:, pl.ds(0, 256)] = q1[:, 128:Q]
    grad_up[:, pl.ds(256, 256)] = q2[:, 0:256]
    grad_down[pl.ds(0, 128), :] = q2[:, 256:Q].T
    grad_down[pl.ds(128, Q), :] = q3.T

    store(grad_gate, grad_gate_out, 3)
    store(grad_up, grad_up_out, 4)
    store(grad_down, grad_down_out, 5)
    ex_dx.arrived()
    for copy in stores:
        copy.wait()
    for copy in started:
        copy.wait_send()


def finish(
    dx_in,
    left_in,
    left_rest_in,
    mixed_in,
    grad_gate_in,
    grad_up_in,
    grad_down_in,
    input_grad_out,
    mixed_out,
    grad_gate_out,
    grad_up_out,
    grad_down_out,
    dx,
    left,
    left_rest,
    input_grad,
    mixed,
    grad_gate,
    grad_up,
    grad_down,
    in_sem,
    out_sem,
):
    rest = pl.ds(J * MAIN, J * REM)
    masks = [
        pltpu.make_async_copy(left_in, left, in_sem.at[5]),
        pltpu.make_async_copy(left_rest_in, left_rest, in_sem.at[6]),
        pltpu.make_async_copy(dx_in.at[:, rest, :], dx.at[:, rest, :], in_sem.at[7]),
    ]
    pieces = []
    for j in range(J):
        rows = pl.ds(j * MAIN, MAIN)
        pieces.append(pltpu.make_async_copy(dx_in.at[:, rows, :], dx.at[:, rows, :], in_sem.at[j]))
    passed = [
        (mixed_in, mixed, mixed_out),
        (grad_gate_in, grad_gate, grad_gate_out),
        (grad_up_in, grad_up, grad_up_out),
        (grad_down_in, grad_down, grad_down_out),
    ]
    taken = [
        pltpu.make_async_copy(src, mid, in_sem.at[8 + n]) for n, (src, mid, _) in enumerate(passed)
    ]
    given = [
        pltpu.make_async_copy(mid, dst, out_sem.at[4 + n]) for n, (_, mid, dst) in enumerate(passed)
    ]
    for copy in masks + pieces + taken:
        copy.start()
    for take, give in zip(taken[0:1], given[0:1]):
        take.wait()
        give.start()
    for copy in masks:
        copy.wait()
    cut = dx[:, rest, :].reshape(E * J * REM, W)
    results = []
    for j in range(J):
        pieces[j].wait()
        rows = dx[:, pl.ds(j * MAIN, MAIN), :].reshape(E * MAIN, W)
        lanes = pl.ds(j * W, W)
        input_grad[:, lanes] = (dot(left[...], rows) + dot(left_rest[j], cut)).astype(BF16)
        result = pltpu.make_async_copy(
            input_grad.at[:, lanes], input_grad_out.at[:, lanes], out_sem.at[j]
        )
        result.start()
        results.append(result)
        if j + 1 < len(taken):
            taken[j + 1].wait()
            given[j + 1].start()
    for copy in given + results:
        copy.wait()


def per_device(tokens, routes, gates, cotangent, w_gate, w_up, w_down):
    vmem = pl.BlockSpec(memory_space=pltpu.VMEM)
    hbm = pl.BlockSpec(memory_space=pl.ANY)
    half = (4, 128, Q)
    outs = (
        jax.ShapeDtypeStruct((T, D), BF16),
        jax.ShapeDtypeStruct((128, H), F32),
        jax.ShapeDtypeStruct((128, H), F32),
        jax.ShapeDtypeStruct((H, 128), F32),
    )
    masks = (
        jax.ShapeDtypeStruct((E, BLK, W), BF16),
        jax.ShapeDtypeStruct((T, E * MAIN), BF16),
        jax.ShapeDtypeStruct((J, T, E * J * REM), BF16),
    )

    def held(shapes):
        return [pltpu.VMEM(s.shape, s.dtype) for s in shapes]

    mixed, dx_back, left, left_rest, gate, up, down = pl.pallas_call(
        kernel,
        out_shape=outs[0:1] + masks + outs[1:],
        in_specs=[vmem] * 2 + [hbm] * 5,
        out_specs=(hbm,) * 7,
        scratch_shapes=[
            pltpu.VMEM((T, D), BF16),
            pltpu.VMEM((T, D), BF16),
            *held(outs),
            *held(masks[1:]),
            pltpu.VMEM((D, 2 * H), BF16),
            pltpu.VMEM((H, D), BF16),
            pltpu.VMEM((E * MAIN, T), BF16),
            pltpu.VMEM((J, E * J * REM, T), BF16),
            pltpu.VMEM((E * MAIN, 2 * T), BF16),
            pltpu.VMEM((J, E * J * REM, 2 * T), BF16),
            pltpu.VMEM((J, E * REM, E * J * REM), BF16),
            pltpu.VMEM((4, E, BLK, W), BF16),
            pltpu.VMEM((2, E, BLK, W), BF16),
            pltpu.VMEM((2, E, BLK, W), BF16),
            pltpu.VMEM((E, BLK, W), BF16),
            pltpu.VMEM((ROWS, D), BF16),
            pltpu.VMEM((ROWS, D), BF16),
            pltpu.VMEM((ROWS, H), F32),
            pltpu.VMEM((ROWS, H), F32),
            pltpu.VMEM((ROWS, H), BF16),
            pltpu.VMEM((ROWS, 2 * H), BF16),
            pltpu.VMEM((E * (MAIN + REM), D), F32),
            pltpu.VMEM((2, E, BLK, W), BF16),
            pltpu.VMEM((2, E, BLK, W), BF16),
            pltpu.VMEM((4, 4, 4, 128, Q), BF16),
            pltpu.VMEM((2, 6) + half, BF16),
            pltpu.VMEM((2, 2) + half, BF16),
            pltpu.VMEM((2, 2) + half, BF16),
            pltpu.VMEM((2, 6, 128, Q), BF16),
            pltpu.VMEM((2, 2, 128, Q), BF16),
            pltpu.SemaphoreType.DMA((5,)),
            pltpu.SemaphoreType.DMA((6,)),
            pltpu.SemaphoreType.DMA((4,)),
            pltpu.SemaphoreType.DMA((56,)),
            pltpu.SemaphoreType.DMA((56,)),
            pltpu.SemaphoreType.REGULAR,
            pltpu.SemaphoreType.REGULAR,
        ],
        compiler_params=pltpu.CompilerParams(
            collective_id=0, has_side_effects=True, vmem_limit_bytes=63_000_000
        ),
        name="moe",
    )(routes.T, gates.T, tokens, cotangent, w_gate, w_up, w_down)
    input_grad, mixed, gate, up, down = pl.pallas_call(
        finish,
        out_shape=outs[0:1] + outs,
        in_specs=[hbm] * 7,
        out_specs=(hbm,) * 5,
        scratch_shapes=[
            *held(masks),
            *held(outs[0:1] + outs),
            pltpu.SemaphoreType.DMA((12,)),
            pltpu.SemaphoreType.DMA((8,)),
        ],
        compiler_params=pltpu.CompilerParams(vmem_limit_bytes=62_000_000),
        name="finish",
    )(dx_back, left, left_rest, mixed, gate, up, down)
    return mixed, input_grad, gate, up, down


def solution(mesh):
    in_specs = (
        P(("dp", "expert"), None),
        P(("dp", "expert"), None),
        P(("dp", "expert"), None),
        P(("dp", "expert"), None),
        P(None, "expert"),
        P(None, "expert"),
        P("expert", None),
    )
    out_specs = (
        P(("dp", "expert"), None),
        P(("dp", "expert"), None),
        P("dp", "expert"),
        P("dp", "expert"),
        P("expert", "dp"),
    )
    return jax.shard_map(
        per_device, mesh=mesh, in_specs=in_specs, out_specs=out_specs, check_vma=False
    )
```
